32 devices in a mesh: row: 8 (over z, y), col: 4 (over x, core).
Axes of the slice: x: 2, y: 2, z: 4, core: 2. Of those that a mesh axis runs over, the one named last changes fastest.
Arguments:
- matrix: float32 [6144, 16384], P('row', 'col'), may hold values from -6 to 6
Outputs:
- updated: float32 [6144, 16384], P('row', 'col')
The draws below stay inside these ranges and needn't reach their ends.
All inputs are finite; a program needn't handle non-finite values.
Results may differ from the reference program's by a relative error of at most 0.0003.
Values sent between devices are 32-bit elements; how exact they have to be, the bound alone decides.
A program may use at most 128 MiB of HBM per device.

```python
import jax
import jax.numpy as jnp
from jax import lax

PANEL = 128
N = 16384
M = 6144


def block_scale(rng, dims, split, least, high):
    loudness, own = 1.0, jax.random.fold_in(rng, 6)
    for axis_at, shards_of in split:
        steps = jnp.exp(jax.random.uniform(jax.random.fold_in(own, axis_at), (shards_of,), jnp.float32, least / len(split), high / len(split)))
        loudness = loudness * jnp.repeat(steps, dims[axis_at] // shards_of).reshape([-1 if axis == axis_at else 1 for axis in range(len(dims))])
    return loudness


def gaussian(own_key, extent, spread, most, cuts=(), kind=jnp.bfloat16):
    drawn = jax.random.normal(own_key, extent, jnp.float32) * spread
    if len(cuts) > 0:
        drawn = block_scale(own_key, extent, cuts, -0.22, 0.18) * drawn
    return jnp.clip(drawn, min=-most, max=most).astype(kind)


def setup_inputs(seed: int = 0) -> dict:
    key_list = jax.random.split(jax.random.key(seed), 2)
    matrix = gaussian(key_list[0], (M, N), 1.0, 6.0, ((0, 8), (1, 4)), jnp.float32)
    return dict(matrix=matrix)


def eliminate(working):
    count = working.shape[0]
    positions = jnp.arange(count).astype(jnp.int32)

    def one_column(column, state):
        pivot_value = state[column, column]
        below = positions > column
        multiplier = jnp.where(below, state[:, column] / pivot_value, jnp.zeros_like(state[:, column]))
        pivot_row = jnp.where(below, state[column, :], jnp.zeros_like(state[column, :]))
        state = state - multiplier[:, None] * pivot_row[None, :]
        return state.at[:, column].set(jnp.where(below, multiplier, state[:, column]))
    result = lax.fori_loop(0, count, one_column, working)
    lower_unit = jnp.tril(result, -1) + jnp.eye(count, dtype=result.dtype)
    upper_tri = jnp.triu(result)
    return (lower_unit, upper_tri)

def reference(matrix):
    high = lax.Precision.HIGHEST
    panel_cols = matrix[:, :PANEL]
    orthonormal, triangle = jnp.linalg.qr(panel_cols)
    sign_fix = jnp.sign(jnp.diagonal(triangle))
    orthonormal = orthonormal * sign_fix[None, :]
    lower_unit, upper_tri = eliminate(orthonormal[:PANEL] + jnp.eye(PANEL, dtype=jnp.float32))
    reflectors = jax.scipy.linalg.solve_triangular(upper_tri.T, orthonormal.T, lower=True)
    reflectors = reflectors.at[:, :PANEL].set(lower_unit.T)
    projected = jnp.dot(reflectors, matrix, precision=high)
    coefficients = jax.scipy.linalg.solve_triangular(lower_unit, jnp.dot(upper_tri.T, projected, precision=high), lower=True, unit_diagonal=True)
    return matrix - jnp.dot(reflectors.T, coefficients, precision=high)
```

```python
import functools

import jax
import jax.numpy as jnp
from jax import lax
from jax.experimental import pallas as pl
from jax.experimental.pallas import tpu as pltpu
from jax.sharding import PartitionSpec as P

PANEL = 128
STRIP = 8
LANES = 128
MESH = pl.DeviceIdType.MESH
EARLY = 4
MIX = 2
END_LAG = 3


def dot_exact(a, b, contract):
    return lax.dot_general(
        a, b, (contract, ((), ())), precision=lax.Precision.HIGHEST, preferred_element_type=jnp.float32
    )


def factor_values(gram, top, between=lambda strip: None):
    strips = PANEL // STRIP
    rows = lax.broadcasted_iota(jnp.int32, (STRIP, 1), 0)
    eye = (
        lax.broadcasted_iota(jnp.int32, (PANEL, PANEL), 0) == lax.broadcasted_iota(jnp.int32, (PANEL, PANEL), 1)
    ).astype(jnp.float32)
    chol = jnp.concatenate([gram, eye], axis=1)
    work = jnp.concatenate([top, jnp.zeros_like(top)], axis=1)
    factor_rows = []
    lanes = lax.broadcasted_iota(jnp.int32, (STRIP, 2 * PANEL), 1)
    previous = None
    for strip in range(strips + 1):
        at, back = strip * STRIP, (strip - 1) * STRIP
        if strip < strips:
            between(strip)
            panel = chol[:STRIP]
            scale = jnp.ones((STRIP, 1), jnp.float32)
        if strip > 0:
            inner = work[back : back + STRIP] + previous
            aside = work[:, back : back + STRIP]
        for j in range(STRIP):
            if strip < strips:
                column = panel[:, at + j : at + j + 1]
                pivot = column[j : j + 1]
                multiplier = jnp.where(rows > j, column / pivot, 0.0)
            if strip > 0:
                inner_column = inner[:, back + j : back + j + 1]
                pivot_row = inner[j : j + 1] / inner_column[j : j + 1]
            if strip < strips:
                scale = jnp.where(rows == j, lax.rsqrt(pivot), scale)
                panel = panel - multiplier * panel[j : j + 1]
            if strip > 0:
                inner = jnp.where(rows == j, pivot_row, inner - inner_column * pivot_row)
        if strip < strips:
            panel = jnp.where(lanes >= at + rows, panel * scale, 0.0)
            factor_rows.append(panel[:, :PANEL])
            if strip < strips - 1:
                chol = chol[STRIP:] - dot_exact(panel[:, at + STRIP : PANEL], panel, ((0,), (0,)))
        if strip > 0:
            update = dot_exact(aside, inner, ((1,), (0,)))
            pieces = []
            if back > 0:
                pieces.append(work[:back] - update[:back])
            pieces.append(inner)
            if strip < strips:
                pieces.append(work[at:] - update[at:])
            work = jnp.concatenate(pieces, axis=0)
        previous = panel
    return jnp.concatenate(factor_rows, axis=0), work[:, PANEL:]


def send(src, dst, send_sem, recv_sem, target):
    return pltpu.make_async_remote_copy(
        src_ref=src, dst_ref=dst, send_sem=send_sem, recv_sem=recv_sem, device_id=target, device_id_type=MESH
    )


def split(x):
    high = x.astype(jnp.bfloat16)
    return high, (x - high.astype(jnp.float32)).astype(jnp.bfloat16)


def step_kernel(
    n_row, n_col, matrix_ref, updated,
    partial, pair_in, chain_in, top_in, hold, stacked, shifted, panel, top, factor_ref, inverse_ref,
    parts, arrived, whole,
    fetch_sem, block_sem, own_sem,
    panel_send, panel_recv, part_send, part_recv, whole_send, whole_recv, top_send, top_recv, share_send, share_recv,
    scatter_send, scatter_recv, pair_send, pair_recv, chain_send, chain_recv,
    give_send, give_recv, pass_send, pass_recv,
):
    row, col = lax.axis_index("row"), lax.axis_index("col")
    width = updated.shape[1]
    blocks = width // (4 * LANES)
    piece = PANEL // n_row
    outer_n = n_row // 2
    last = outer_n - 1
    outer, inner = row // 2, lax.rem(row, 2)
    other = 1 - inner
    partner = {"row": outer * 2 + other}
    first, final = outer == 0, outer == last
    is_end = first | final
    mine = jnp.where(first, 0, 1)
    near = jnp.where(2 * outer < outer_n, 0, 1)
    far = 1 - near
    end_rows = [0, 1, n_row - 2, n_row - 1]

    barrier = pltpu.get_barrier_semaphore()
    for d in range(1, n_row):
        pl.semaphore_signal(barrier, inc=1, device_id={"row": lax.rem(row + d, n_row)}, device_id_type=MESH)
    for d in range(1, n_col):
        pl.semaphore_signal(barrier, inc=1, device_id={"col": lax.rem(col + d, n_col)}, device_id_type=MESH)

    def lanes(start, size):
        return pl.ds(pl.multiple_of(start, LANES), size)

    def unit(p, side):
        return lanes(p * (2 * LANES) + side * LANES, LANES)

    def load(j):
        place = lanes(j * (4 * LANES), 4 * LANES)
        return pltpu.make_async_copy(matrix_ref.at[:, place], updated.at[:, place], block_sem.at[j])

    def scatter(i, e):
        row_to = end_rows[e]
        place = unit(2 * i + e // 2, e % 2)
        return send(
            matrix_ref.at[pl.ds(0, PANEL), place], top_in.at[i], scatter_send.at[i, e], scatter_recv.at[i],
            {"row": row_to},
        )

    def keep(i):
        return pltpu.make_async_copy(matrix_ref.at[pl.ds(0, PANEL), unit(2 * i, 0)], top_in.at[i], own_sem.at[i])

    def start_scatter(i):
        @pl.when(row == 0)
        def _():
            for e in range(1, 4):
                scatter(i, e).start()

    def pair(p):
        return send(partial.at[:, unit(p, other)], pair_in.at[p], pair_send.at[p], pair_recv.at[p], partner)

    def chain(p, towards, own):
        slot = 0 if own else 1
        return send(
            partial.at[:, unit(p, inner if own else other)], chain_in.at[p, slot],
            chain_send.at[p, slot], chain_recv.at[p, slot], {"row": row + 2 * (2 * towards - 1)},
        )

    def is_direct(i, owner):
        return (owner == 1) & (lax.rem(i, MIX) != 0)

    def joins(owner):
        return outer == jnp.where(owner == 0, 1, last - 1)

    def owns(owner):
        return is_end & (owner == mine)

    def leads(owner):
        return is_end & (owner != mine)

    def give(p):
        place = unit(p, inner)
        return send(hold.at[:, place], hold.at[:, place], give_send.at[p], give_recv.at[p], partner)

    def given(p):
        place = unit(p, other)
        return send(hold.at[:, place], hold.at[:, place], give_send.at[p], give_recv.at[p], partner)

    def onward(p, owner, own):
        place = unit(p, inner if own else other)
        slot = 0 if own else 1
        return send(
            hold.at[:, place], hold.at[:, place], pass_send.at[p, slot], pass_recv.at[p, slot],
            {"row": row + 2 * (1 - 2 * owner)},
        )

    def multiply(j):
        place = lanes(j * (4 * LANES), 4 * LANES)
        high, low = split(updated[:, place])
        both = jnp.dot(stacked[...], high, preferred_element_type=jnp.float32)
        rest = jnp.dot(stacked[:PANEL], low, preferred_element_type=jnp.float32)
        partial[:, place] = both[:PANEL] + both[PANEL:] + rest

    def exchange(i):
        for side in range(2):
            p = 2 * i + side

            @pl.when(owns(side))
            def _():
                pair(p).start()

            @pl.when(leads(side))
            def _():
                chain(p, side, True).start()
                chain(p, side, False).start()

    def prepare():
        high, low = split(panel[...])
        shifted[:, :PANEL] = high
        shifted[:, PANEL:] = low
        high, low = split(jnp.transpose(panel[...]))
        stacked[:PANEL] = high
        stacked[PANEL:] = low

    def multiply_range(start, stop, ahead):
        @pl.loop(start, stop)
        def _(j):
            load(j).wait()
            multiply(j)
            exchange(j)

            @pl.when(j + ahead < blocks)
            def _():
                start_scatter(j + ahead)

    @pl.when(col == 0)
    def _():
        fetch = pltpu.make_async_copy(matrix_ref.at[:, pl.ds(0, PANEL)], panel, fetch_sem.at[0])
        fetch.start()
        fetch.wait()
        for j in range(blocks):
            load(j).start()
        local = dot_exact(panel[...], panel[...], ((0,), (0,)))
        for q in range(n_row):
            parts[q] = local[q * piece : (q + 1) * piece]

    @pl.when(col != 0)
    def _():
        for j in range(blocks):
            load(j).start()

    @pl.when(row == 0)
    def _():
        for i in range(blocks):
            keep(i).start()

    pl.semaphore_wait(barrier, n_row - 1 + n_col - 1)

    def panel_copy(to, slot):
        return send(panel, panel, panel_send.at[slot], panel_recv.at[0], {"col": to})

    heads = [1] + [c for c in range(2, n_col, 2)]

    @pl.when(col == 0)
    def _():
        def part(d):
            q = lax.rem(row + d, n_row)
            return send(parts.at[q], arrived.at[d - 1], part_send.at[d - 1], part_recv.at[d - 1], {"row": q})

        def whole_copy(e):
            return send(whole.at[row], whole.at[row], whole_send.at[e], whole_recv.at[row], {"row": end_rows[e]})

        def top_copy(e):
            return send(panel.at[pl.ds(0, PANEL)], top, top_send.at[e], top_recv.at[0], {"row": end_rows[e]})

        def share(c, slot):
            ref = (top, whole)[slot]
            return send(ref, ref, share_send.at[c - 1, slot], share_recv.at[slot], {"col": c})

        for d in range(1, n_row):
            part(d).start()
        for slot, c in enumerate(heads[1:]):
            panel_copy(c, slot + 1).start()

        @pl.when(row == 0)
        def _():
            for e in range(1, 4):
                top_copy(e).start()
            top[...] = panel[:PANEL]

        prepare()

        @pl.loop(0, blocks // 2)
        def _(j):
            load(j).wait()
            multiply(j)

        total = parts[row]
        for d in range(1, n_row):
            part(d).wait_recv()
            total = total + arrived[d - 1]
        whole[row] = total
        for e in range(4):
            @pl.when(row != end_rows[e])
            def _():
                whole_copy(e).start()

        panel_copy(heads[0], 0).start()

        @pl.loop(0, blocks // 2)
        def _(j):
            exchange(j)
            start_scatter(j)

        @pl.when(is_end)
        def _():
            @pl.when(row != 0)
            def _():
                send(top, top, top_send.at[0], top_recv.at[0], {"row": 0}).wait_recv()

            for c in range(1, n_col):
                share(c, 0).start()

        multiply_range(blocks // 2, blocks, 0)

        @pl.when(is_end)
        def _():
            for q in range(n_row):
                @pl.when(row != q)
                def _():
                    send(whole.at[q], whole.at[q], whole_send.at[0], whole_recv.at[q], {"row": q}).wait_recv()
            for c in range(1, n_col):
                share(c, 1).start()
            for c in range(1, n_col):
                share(c, 0).wait_send()
                share(c, 1).wait_send()

        for d in range(1, n_row):
            part(d).wait_send()
        for slot, c in enumerate(heads):
            panel_copy(c, slot).wait_send()
        for e in range(4):
            @pl.when(row != end_rows[e])
            def _():
                whole_copy(e).wait_send()

        @pl.when(row == 0)
        def _():
            for e in range(1, 4):
                top_copy(e).wait_send()

    @pl.when(col != 0)
    def _():
        for i in range(EARLY):
            @pl.when(col != 1)
            def _():
                start_scatter(i)
        root = {"col": 0}
        send(panel, panel, panel_send.at[0], panel_recv.at[0], root).wait_recv()
        relay = (lax.rem(col, 2) == 0) & (col + 1 < n_col)

        @pl.when(relay)
        def _():
            panel_copy(col + 1, 0).start()

        prepare()
        ahead = jnp.where(col == 1, 0, EARLY)
        multiply_range(0, blocks, ahead)

        @pl.when(is_end)
        def _():
            send(top, top, share_send.at[0, 0], share_recv.at[0], root).wait_recv()
            send(whole, whole, share_send.at[0, 1], share_recv.at[1], root).wait_recv()

        @pl.when(relay)
        def _():
            panel_copy(col + 1, 0).wait_send()

    def add(p, side, *terms):
        place = unit(p, side)
        total = partial[:, place]
        for term in terms:
            total = total + term[...]
        partial[:, place] = total

    def relay_sum(i, owner):
        p = 2 * i + owner
        chain(p, owner, True).wait_recv()
        add(p, inner, chain_in.at[p, 0])

        @pl.when(jnp.logical_not(joins(owner)))
        def _():
            chain(p, owner, True).start()

        chain(p, owner, False).wait_recv()
        add(p, other, chain_in.at[p, 1])

        @pl.when(joins(owner))
        def _():
            pair(p).start()

        @pl.when(jnp.logical_not(joins(owner)))
        def _():
            chain(p, owner, False).start()

    def join_sum(i, owner):
        @pl.when(joins(owner))
        def _():
            p = 2 * i + owner
            pair(p).wait_recv()
            add(p, inner, pair_in.at[p])
            chain(p, owner, True).start()

    @pl.when(is_end)
    def _():
        gram = jnp.concatenate([whole[q] for q in range(n_row)], axis=0)

        factor, inverse = factor_values(gram, top[...])
        factor_ref[...] = factor
        inverse_ref[:, :PANEL] = inverse
        inverse_ref[:, PANEL:] = dot_exact(inverse, factor, ((1,), (1,)))

        @pl.when(row == 0)
        def _():
            high, low = split(panel[:PANEL] + factor)
            shifted[:PANEL, :PANEL] = high
            shifted[:PANEL, PANEL:] = low

    @pl.when(jnp.logical_not(is_end))
    def _():
        @pl.loop(0, blocks + 2)
        def _(s):
            @pl.when(s >= 2)
            def _():
                join_sum(s - 2, near)

            @pl.when(s < blocks)
            def _():
                relay_sum(s, far)

            @pl.when((s >= 1) & (s <= blocks))
            def _():
                relay_sum(s - 1, near)

    def update(p):
        place = lanes(p * (2 * LANES), 2 * LANES)
        high, low = split(hold[:, place])
        both = jnp.dot(shifted[...], jnp.concatenate([high, high], axis=0), preferred_element_type=jnp.float32)
        rest = jnp.dot(shifted[:, :PANEL], low, preferred_element_type=jnp.float32)
        updated[:, place] = updated[:, place] - (both + rest)

    def solve(i):
        p = 2 * i + mine
        pair(p).wait_recv()
        chain(p, mine, True).wait_recv()

        @pl.when(row == 0)
        def _():
            keep(i).wait()

        @pl.when(row != 0)
        def _():
            send(top_in.at[i], top_in.at[i], scatter_send.at[i, 0], scatter_recv.at[i], {"row": 0}).wait_recv()

        place = unit(p, inner)
        total = partial[:, place] + pair_in[p] + chain_in[p, 0]
        hold[:, place] = dot_exact(inverse_ref[...], jnp.concatenate([total, top_in[i]], axis=0), ((1,), (0,)))
        onward(p, mine, True).start()
        give(p).start()

    def pass_other(i):
        p = 2 * i + mine

        @pl.when(is_direct(i, mine))
        def _():
            given(p).wait_recv()
            onward(p, mine, False).start()

    def accept(i, owner):
        p = 2 * i + owner
        stops = jnp.where(owner == 0, final, first)
        onward(p, owner, True).wait_recv()

        @pl.when(jnp.logical_not(stops))
        def _():
            onward(p, owner, True).start()

        @pl.when(is_direct(i, owner))
        def _():
            onward(p, owner, False).wait_recv()

            @pl.when(jnp.logical_not(stops))
            def _():
                onward(p, owner, False).start()

        @pl.when(jnp.logical_not(is_direct(i, owner)))
        def _():
            give(p).start()

    def finish(i, owner):
        p = 2 * i + owner

        @pl.when(jnp.logical_not(is_direct(i, owner)))
        def _():
            given(p).wait_recv()

        update(p)

    @pl.when(is_end)
    def _():
        @pl.loop(0, blocks + 2)
        def _(i):
            @pl.when(i < blocks)
            def _():
                solve(i)

            @pl.when(i >= 2)
            def _():
                pass_other(i - 2)

    def settle_sums(i, side):
        p = 2 * i + side

        @pl.when(owns(side) | joins(side))
        def _():
            pair(p).wait_send()

        @pl.when(jnp.logical_not(owns(side)))
        def _():
            chain(p, side, True).wait_send()

        @pl.when(jnp.logical_not(owns(side) | joins(side)))
        def _():
            chain(p, side, False).wait_send()

    def settle_back(i, side):
        p = 2 * i + side

        @pl.when(jnp.logical_not(leads(side)))
        def _():
            onward(p, side, True).wait_send()

            @pl.when(is_direct(i, side))
            def _():
                onward(p, side, False).wait_send()

        @pl.when(owns(side) | jnp.logical_not(is_direct(i, side)))
        def _():
            give(p).wait_send()

    wait = jnp.where(is_end, 0, 2)
    lag = jnp.where(is_end, END_LAG, 1)

    @pl.loop(0, blocks + END_LAG + 2)
    def _(s):
        @pl.when(s < blocks)
        def _():
            for side in range(2):
                settle_sums(s, side)

            @pl.when(row == 0)
            def _():
                for e in range(1, 4):
                    scatter(s, e).wait_send()

        @pl.when((s >= wait) & (s < blocks + wait))
        def _():
            finish(s - wait, near)

        @pl.when(jnp.logical_not(is_end) & (s < blocks))
        def _():
            accept(s, near)

        @pl.when((s >= lag + 2) & (s < blocks + lag + 2))
        def _():
            finish(s - lag - 2, far)

        @pl.when((s >= lag) & (s < blocks + lag))
        def _():
            accept(s - lag, far)

    @pl.loop(0, blocks)
    def _(i):
        for side in range(2):
            settle_back(i, side)


def flush_kernel(ready, out, sem):
    pieces = sem.shape[0]
    rows = out.shape[0] // pieces
    copies = [
        pltpu.make_async_copy(ready.at[pl.ds(q * rows, rows)], out.at[pl.ds(q * rows, rows)], sem.at[q])
        for q in range(pieces)
    ]
    for copy in copies:
        copy.start()
    for copy in copies:
        copy.wait()


def flush(ready):
    return pl.pallas_call(
        flush_kernel,
        out_shape=jax.ShapeDtypeStruct(ready.shape, ready.dtype),
        in_specs=[pl.BlockSpec(memory_space=pltpu.VMEM)],
        out_specs=pl.BlockSpec(memory_space=pl.ANY),
        scratch_shapes=[pltpu.SemaphoreType.DMA((8,))],
        compiler_params=pltpu.CompilerParams(vmem_limit_bytes=16 * 1024 * 1024),
        name="flush",
    )(ready)


def on_device(n_row, n_col, matrix):
    height, width = matrix.shape
    piece = PANEL // n_row
    blocks = width // (4 * LANES)
    pairs = 2 * blocks
    dma = pltpu.SemaphoreType.DMA
    f32, bf16 = jnp.float32, jnp.bfloat16
    ready = pl.pallas_call(
        functools.partial(step_kernel, n_row, n_col),
        out_shape=jax.ShapeDtypeStruct((height, width), f32),
        in_specs=[pl.BlockSpec(memory_space=pl.ANY)],
        out_specs=pl.BlockSpec(memory_space=pltpu.VMEM),
        scratch_shapes=[
            pltpu.VMEM((PANEL, width), f32),
            pltpu.VMEM((pairs, PANEL, LANES), f32),
            pltpu.VMEM((pairs, 2, PANEL, LANES), f32),
            pltpu.VMEM((blocks, PANEL, LANES), f32),
            pltpu.VMEM((PANEL, width), f32),
            pltpu.VMEM((2 * PANEL, height), bf16),
            pltpu.VMEM((height, 2 * PANEL), bf16),
            pltpu.VMEM((height, PANEL), f32),
            pltpu.VMEM((PANEL, PANEL), f32),
            pltpu.VMEM((PANEL, PANEL), f32),
            pltpu.VMEM((PANEL, 2 * PANEL), f32),
            pltpu.VMEM((n_row, piece, PANEL), f32),
            pltpu.VMEM((n_row - 1, piece, PANEL), f32),
            pltpu.VMEM((n_row, piece, PANEL), f32),
            dma((1,)),
            dma((blocks,)),
            dma((blocks,)),
            dma((n_col,)),
            dma((1,)),
            dma((n_row - 1,)),
            dma((n_row - 1,)),
            dma((4,)),
            dma((n_row,)),
            dma((4,)),
            dma((1,)),
            dma((n_col - 1, 2)),
            dma((2,)),
            dma((blocks, 4)),
            dma((blocks,)),
            dma((pairs,)),
            dma((pairs,)),
            dma((pairs, 2)),
            dma((pairs, 2)),
            dma((pairs,)),
            dma((pairs,)),
            dma((pairs, 2)),
            dma((pairs, 2)),
        ],
        compiler_params=pltpu.CompilerParams(
            collective_id=0, has_side_effects=True, vmem_limit_bytes=40 * 1024 * 1024
        ),
        name="whole_step",
    )(matrix)
    return flush(ready)


def solution(mesh):
    body = functools.partial(on_device, mesh.shape["row"], mesh.shape["col"])
    return jax.shard_map(body, mesh=mesh, in_specs=(P("row", "col"),), out_specs=P("row", "col"), check_vma=False)
```

```python
import functools

import jax
import jax.numpy as jnp
from jax import lax
from jax.experimental import pallas as pl
from jax.experimental.pallas import tpu as pltpu
from jax.sharding import PartitionSpec as P

PANEL = 128
STRIP = 8
LANES = 128
MESH = pl.DeviceIdType.MESH
EARLY = 8
EARLY_UP = 4
LATE = 3
MIX = 4
LEAD_PACE = 1.4
HOP = 3.2


def dot_exact(a, b, contract):
    return lax.dot_general(
        a, b, (contract, ((), ())), precision=lax.Precision.HIGHEST, preferred_element_type=jnp.float32
    )


def factor_values(gram, top, between=lambda strip: None):
    strips = PANEL // STRIP
    rows = lax.broadcasted_iota(jnp.int32, (STRIP, 1), 0)
    eye = (
        lax.broadcasted_iota(jnp.int32, (PANEL, PANEL), 0) == lax.broadcasted_iota(jnp.int32, (PANEL, PANEL), 1)
    ).astype(jnp.float32)
    chol = jnp.concatenate([gram, eye], axis=1)
    work = jnp.concatenate([top, jnp.zeros_like(top)], axis=1)
    factor_rows = []
    lanes = lax.broadcasted_iota(jnp.int32, (STRIP, 2 * PANEL), 1)
    previous = None
    for strip in range(strips + 1):
        at, back = strip * STRIP, (strip - 1) * STRIP
        if strip < strips:
            between(strip)
            panel = chol[:STRIP]
            scale = jnp.ones((STRIP, 1), jnp.float32)
        if strip > 0:
            inner = work[back : back + STRIP] + previous
            aside = work[:, back : back + STRIP]
        for j in range(STRIP):
            if strip < strips:
                column = panel[:, at + j : at + j + 1]
                pivot = column[j : j + 1]
                multiplier = jnp.where(rows > j, column / pivot, 0.0)
            if strip > 0:
                inner_column = inner[:, back + j : back + j + 1]
                pivot_row = inner[j : j + 1] / inner_column[j : j + 1]
            if strip < strips:
                scale = jnp.where(rows == j, lax.rsqrt(pivot), scale)
                panel = panel - multiplier * panel[j : j + 1]
            if strip > 0:
                inner = jnp.where(rows == j, pivot_row, inner - inner_column * pivot_row)
        if strip < strips:
            panel = jnp.where(lanes >= at + rows, panel * scale, 0.0)
            factor_rows.append(panel[:, :PANEL])
            if strip < strips - 1:
                chol = chol[STRIP:] - dot_exact(panel[:, at + STRIP : PANEL], panel, ((0,), (0,)))
        if strip > 0:
            update = dot_exact(aside, inner, ((1,), (0,)))
            pieces = []
            if back > 0:
                pieces.append(work[:back] - update[:back])
            pieces.append(inner)
            if strip < strips:
                pieces.append(work[at:] - update[at:])
            work = jnp.concatenate(pieces, axis=0)
        previous = panel
    return jnp.concatenate(factor_rows, axis=0), work[:, PANEL:]


def send(src, dst, send_sem, recv_sem, target):
    return pltpu.make_async_remote_copy(
        src_ref=src, dst_ref=dst, send_sem=send_sem, recv_sem=recv_sem, device_id=target, device_id_type=MESH
    )


def split(x):
    high = x.astype(jnp.bfloat16)
    return high, (x - high.astype(jnp.float32)).astype(jnp.bfloat16)


def owned_counts(pairs):
    return pairs - pairs // 3, pairs // 3


def is_direct(i, owner):
    return owner == 1 or i % MIX == MIX - 1


def plan(role, counts):
    events = []

    def put(time, kind, owner, i):
        events.append((time, len(events), (kind, owner, i)))

    for i in range(counts[0]):
        solved = max(36.5 + 0.4 * i, 25.5 + 1.5 * i)
        sent = max(37.0 + 1.4 * i, solved)
        if role == 0:
            put(solved, "solve", 0, i)
            if is_direct(i, 0):
                put(sent + HOP, "pass", 0, i)
        else:
            put(sent + HOP * role, "own", 0, i)
            if is_direct(i, 0):
                put(sent + HOP * (role + 1), "other", 0, i)
        if role in (1, 2):
            put(18.3 + 1.5 * i + HOP * (2 - role), "down", 0, i)
    for i in range(counts[1]):
        solved = 32.6 + 2.75 * i
        if role == 3:
            put(solved, "solve", 1, i)
            put(solved + HOP, "pass", 1, i)
        else:
            put(solved + HOP * (3 - role), "own", 1, i)
            put(solved + HOP * (4 - role), "other", 1, i)
        late = role == 2 and i == counts[1] - 1
        if role in (1, 2):
            put(36.5 if late else 13.0 + 2.8 * i + HOP * (role - 1), "up", 1, i)
        if role == 2:
            put(39.7 if late else 20.0 + 2.8 * i, "join", 1, i)
    put(46.0, "sums", 0, 0)
    return [event for _, _, event in sorted(events)]


def step_kernel(
    n_row, n_col, matrix_ref, updated, hold, shifted,
    partial, pair_in, chain_in, top_in, stacked, panel, top, factor_ref, inverse_ref,
    parts, arrived, whole,
    fetch_sem, block_sem, own_sem,
    panel_send, panel_recv, part_send, part_recv, whole_send, whole_recv, top_send, top_recv, share_send, share_recv,
    scatter_send, scatter_recv, pair_send, pair_recv, chain_send, chain_recv,
    give_send, give_recv, pass_send, pass_recv,
):
    row, col = lax.axis_index("row"), lax.axis_index("col")
    width = updated.shape[1]
    blocks = width // (4 * LANES)
    pairs = 2 * blocks
    counts = owned_counts(pairs)
    prompt = pairs - LATE
    piece = PANEL // n_row
    outer_n = n_row // 2
    last = outer_n - 1
    outer, inner = row // 2, lax.rem(row, 2)
    other = 1 - inner
    partner = {"row": outer * 2 + other}
    first, final = outer == 0, outer == last
    is_end = first | final
    mine = jnp.where(first, 0, 1)
    near = jnp.where(2 * outer < outer_n, 0, 1)
    end_rows = [0, 1, n_row - 2, n_row - 1]

    barrier = pltpu.get_barrier_semaphore()
    for d in range(1, n_row):
        pl.semaphore_signal(barrier, inc=1, device_id={"row": lax.rem(row + d, n_row)}, device_id_type=MESH)
    for d in range(1, n_col):
        pl.semaphore_signal(barrier, inc=1, device_id={"col": lax.rem(col + d, n_col)}, device_id_type=MESH)

    def lanes(start, size):
        return pl.ds(pl.multiple_of(start, LANES), size)

    def unit(p, side):
        return lanes(p * (2 * LANES) + side * LANES, LANES)

    def load(j):
        place = lanes(j * (4 * LANES), 4 * LANES)
        return pltpu.make_async_copy(matrix_ref.at[:, place], updated.at[:, place], block_sem.at[j])

    def static_slot(i, owner):
        return i + i // 2 if owner == 0 else 3 * i + 2

    def owner_of(p):
        return jnp.where(lax.rem(p, 3) == 2, 1, 0)

    def turn_of(p):
        return jnp.where(lax.rem(p, 3) == 2, lax.div(p, 3), p - lax.div(p, 3))

    def scatter(p, side, up):
        return send(
            matrix_ref.at[pl.ds(0, PANEL), unit(p, side)], top_in.at[turn_of(p)],
            scatter_send.at[p, side], scatter_recv.at[turn_of(p)], {"row": end_rows[2 * up + side]},
        )

    def keep(i):
        place = unit(static_slot(i, 0), 0)
        return pltpu.make_async_copy(matrix_ref.at[pl.ds(0, PANEL), place], top_in.at[i], own_sem.at[i])

    def start_scatter(p):
        @pl.when((row == 0) & (owner_of(p) == 0) & (p < prompt))
        def _():
            scatter(p, 1, 0).start()

    def start_up(i):
        @pl.when(row == 0)
        def _():
            for side in range(2):
                scatter(static_slot(i, 1), side, 1).start()

    def pair(p):
        return send(partial.at[:, unit(p, other)], pair_in.at[p], pair_send.at[p], pair_recv.at[p], partner)

    def chain(p, towards, own):
        slot = 0 if own else 1
        return send(
            partial.at[:, unit(p, inner if own else other)], chain_in.at[p, slot],
            chain_send.at[p, slot], chain_recv.at[p, slot], {"row": row + 2 * (2 * towards - 1)},
        )

    joins = outer == last - 1

    def is_held(p):
        return (owner_of(p) == 0) & (p >= prompt)

    def give(p):
        place = unit(p, inner)
        return send(hold.at[:, place], hold.at[:, place], give_send.at[p], give_recv.at[p], partner)

    def given(p):
        place = unit(p, other)
        return send(hold.at[:, place], hold.at[:, place], give_send.at[p], give_recv.at[p], partner)

    def onward(p, owner, own):
        place = unit(p, inner if own else other)
        slot = 0 if own else 1
        return send(
            hold.at[:, place], hold.at[:, place], pass_send.at[p, slot], pass_recv.at[p, slot],
            {"row": row + 2 * (1 - 2 * owner)},
        )

    def multiply(j):
        place = lanes(j * (4 * LANES), 4 * LANES)
        high, low = split(updated[:, place])
        both = jnp.dot(stacked[...], high, preferred_element_type=jnp.float32)
        rest = jnp.dot(stacked[:PANEL], low, preferred_element_type=jnp.float32)
        partial[:, place] = both[:PANEL] + both[PANEL:] + rest

    def exchange(p):
        owner = owner_of(p)

        @pl.when((owner == 0) & jnp.logical_not((row == 0) & is_held(p)))
        def _():
            pair(p).start()

        @pl.when((owner == 1) & first)
        def _():
            chain(p, owner, True).start()
            chain(p, owner, False).start()

    def exchange_last():
        @pl.when(final)
        def _():
            for i in range(counts[1]):
                pair(static_slot(i, 1)).start()

    def prepare():
        high, low = split(panel[...])
        shifted[:, :PANEL] = high
        shifted[:, PANEL:] = low
        high, low = split(jnp.transpose(panel[...]))
        stacked[:PANEL] = high
        stacked[PANEL:] = low

    def multiply_range(start, stop, ahead):
        @pl.loop(start, stop)
        def _(j):
            load(j).wait()
            multiply(j)
            for p in (2 * j, 2 * j + 1):
                exchange(p)

                @pl.when(p + ahead < pairs)
                def _():
                    start_scatter(p + ahead)

    @pl.when(col == 0)
    def _():
        fetch = pltpu.make_async_copy(matrix_ref.at[:, pl.ds(0, PANEL)], panel, fetch_sem.at[0])
        fetch.start()
        fetch.wait()
        for j in range(blocks):
            load(j).start()
        local = dot_exact(panel[...], panel[...], ((0,), (0,)))
        for q in range(n_row):
            parts[q] = local[q * piece : (q + 1) * piece]

    @pl.when(col != 0)
    def _():
        for j in range(blocks):
            load(j).start()

    @pl.when(row == 0)
    def _():
        for i in range(counts[0]):
            if static_slot(i, 0) < prompt:
                keep(i).start()

    pl.semaphore_wait(barrier, n_row - 1 + n_col - 1)

    def panel_copy(to, slot):
        return send(panel, panel, panel_send.at[slot], panel_recv.at[0], {"col": to})

    heads = [1] + [c for c in range(2, n_col, 2)]

    @pl.when(col == 0)
    def _():
        def part(d):
            q = lax.rem(row + d, n_row)
            return send(parts.at[q], arrived.at[d - 1], part_send.at[d - 1], part_recv.at[d - 1], {"row": q})

        def whole_copy(e):
            return send(whole.at[row], whole.at[row], whole_send.at[e], whole_recv.at[row], {"row": end_rows[e]})

        def top_copy(e):
            return send(panel.at[pl.ds(0, PANEL)], top, top_send.at[e], top_recv.at[0], {"row": end_rows[e]})

        def share(c, slot):
            ref = (top, whole)[slot]
            return send(ref, ref, share_send.at[c - 1, slot], share_recv.at[slot], {"col": c})

        for d in range(1, n_row):
            part(d).start()
        for slot, c in enumerate(heads[1:]):
            panel_copy(c, slot + 1).start()

        @pl.when(row == 0)
        def _():
            for e in range(1, 4):
                top_copy(e).start()
            top[...] = panel[:PANEL]

        prepare()

        @pl.loop(0, blocks // 2)
        def _(j):
            load(j).wait()
            multiply(j)

        total = parts[row]
        for d in range(1, n_row):
            part(d).wait_recv()
            total = total + arrived[d - 1]
        whole[row] = total
        for e in range(4):
            @pl.when(row != end_rows[e])
            def _():
                whole_copy(e).start()

        panel_copy(heads[0], 0).start()

        @pl.loop(0, 2 * (blocks // 2))
        def _(p):
            exchange(p)

            start_scatter(p)

        @pl.when(is_end)
        def _():
            @pl.when(row != 0)
            def _():
                send(top, top, top_send.at[0], top_recv.at[0], {"row": 0}).wait_recv()

            for c in range(1, n_col):
                share(c, 0).start()

        multiply_range(blocks // 2, blocks, 0)
        exchange_last()
        for i in range(counts[1]):
            start_up(i)

        @pl.when(is_end)
        def _():
            for q in range(n_row):
                @pl.when(row != q)
                def _():
                    send(whole.at[q], whole.at[q], whole_send.at[0], whole_recv.at[q], {"row": q}).wait_recv()
            for c in range(1, n_col):
                share(c, 1).start()
            for c in range(1, n_col):
                share(c, 0).wait_send()
                share(c, 1).wait_send()

        for d in range(1, n_row):
            part(d).wait_send()
        for slot, c in enumerate(heads):
            panel_copy(c, slot).wait_send()
        for e in range(4):
            @pl.when(row != end_rows[e])
            def _():
                whole_copy(e).wait_send()

        @pl.when(row == 0)
        def _():
            for e in range(1, 4):
                top_copy(e).wait_send()

    @pl.when(col != 0)
    def _():
        @pl.when(col != 1)
        def _():
            for p in range(EARLY):
                start_scatter(p)
            for i in range(EARLY_UP):
                start_up(i)

        root = {"col": 0}
        send(panel, panel, panel_send.at[0], panel_recv.at[0], root).wait_recv()
        relay = (lax.rem(col, 2) == 0) & (col + 1 < n_col)

        @pl.when(relay)
        def _():
            panel_copy(col + 1, 0).start()

        prepare()
        ahead = jnp.where(col == 1, 0, EARLY)
        multiply_range(0, blocks, ahead)
        exchange_last()

        for i in range(counts[1]):
            @pl.when((col == 1) | (i >= EARLY_UP))
            def _():
                start_up(i)

        @pl.when(is_end)
        def _():
            send(top, top, share_send.at[0, 0], share_recv.at[0], root).wait_recv()
            send(whole, whole, share_send.at[0, 1], share_recv.at[1], root).wait_recv()

        @pl.when(relay)
        def _():
            panel_copy(col + 1, 0).wait_send()

    def add(p, side, *terms):
        place = unit(p, side)
        total = partial[:, place]
        for term in terms:
            total = total + term[...]
        partial[:, place] = total

    def lead(i):
        p = static_slot(i, 0)
        pair(p).wait_recv()
        add(p, inner, pair_in.at[p])
        chain(p, 0, True).start()

    def relay_down(i):
        p = static_slot(i, 0)
        pair(p).wait_recv()
        chain(p, 0, True).wait_recv()
        add(p, inner, pair_in.at[p], chain_in.at[p, 0])
        chain(p, 0, True).start()

    def relay_up(i):
        p = static_slot(i, 1)
        for own in (False, True):
            chain(p, 1, own).wait_recv()
            add(p, inner if own else other, chain_in.at[p, 0 if own else 1])

            @pl.when(jnp.logical_not(joins))
            def _():
                chain(p, 1, own).start()

            if not own:
                @pl.when(joins)
                def _():
                    pair(p).start()

    def join_up(i):
        @pl.when(joins)
        def _():
            p = static_slot(i, 1)
            pair(p).wait_recv()
            add(p, inner, pair_in.at[p])
            chain(p, 1, True).start()

    @pl.when(is_end)
    def _():
        gram = jnp.concatenate([whole[q] for q in range(n_row)], axis=0)

        strips = [2 + int(LEAD_PACE * i) for i in range(counts[0])]

        def between(strip):
            if strip in strips:
                @pl.when(final)
                def _():
                    lead(strips.index(strip))

        factor, inverse = factor_values(gram, top[...], between)
        factor_ref[...] = factor
        inverse_ref[:, :PANEL] = inverse
        inverse_ref[:, PANEL:] = dot_exact(inverse, factor, ((1,), (1,)))

        @pl.when(final)
        def _():
            for i in range(counts[0]):
                if strips[i] >= PANEL // STRIP:
                    lead(i)

        @pl.when(row == 0)
        def _():
            high, low = split(panel[:PANEL] + factor)
            shifted[:PANEL, :PANEL] = high
            shifted[:PANEL, PANEL:] = low

            for p in range(prompt, pairs):
                if p % 3 != 2:
                    place = lanes(p * (2 * LANES) + LANES, LANES)
                    extra = dot_exact(factor, updated[:PANEL, place], ((0,), (0,)))
                    partial[:, place] = partial[:, place] + extra
                    pair(p).start()

    def solve(i, owner):
        p = static_slot(i, owner)
        pair(p).wait_recv()
        chain(p, owner, True).wait_recv()
        place = unit(p, inner)
        held = owner == 0 and p >= prompt

        def at_row_zero():
            if held:
                top_in[i] = updated[:PANEL, place]
            else:
                keep(i).wait()

        def elsewhere():
            if held:
                top_in[i] = jnp.zeros((PANEL, LANES), jnp.float32)
            else:
                send(top_in.at[i], top_in.at[i], scatter_send.at[0, 0], scatter_recv.at[i], {"row": 0}).wait_recv()

        if owner == 0:
            pl.when(row == 0)(at_row_zero)
            pl.when(row != 0)(elsewhere)
        else:
            elsewhere()
        total = partial[:, place] + pair_in[p] + chain_in[p, 0]
        hold[:, place] = dot_exact(inverse_ref[...], jnp.concatenate([total, top_in[i]], axis=0), ((1,), (0,)))
        onward(p, owner, True).start()
        give(p).start()

    def pass_other(i, owner):
        p = static_slot(i, owner)
        given(p).wait_recv()
        onward(p, owner, False).start()

    def accept(i, owner, own, stops):
        p = static_slot(i, owner)
        onward(p, owner, own).wait_recv()
        if not stops:
            onward(p, owner, own).start()
        if own and not is_direct(i, owner):
            give(p).start()

    def settle_sums(role):
        for p in range(pairs):
            owner = 1 if p % 3 == 2 else 0
            if owner == 0:
                pair(p).wait_send()
                if role != 0:
                    chain(p, 0, True).wait_send()
            elif role == 0:
                chain(p, 1, True).wait_send()
                chain(p, 1, False).wait_send()
            elif role == 3:
                pair(p).wait_send()
            else:
                chain(p, 1, True).wait_send()

                @pl.when(joins)
                def _():
                    pair(p).wait_send()

                @pl.when(jnp.logical_not(joins))
                def _():
                    chain(p, 1, False).wait_send()
        if role == 0:
            @pl.when(row == 0)
            def _():
                for p in range(pairs):
                    if p % 3 == 2:
                        scatter(p, 0, 1).wait_send()
                        scatter(p, 1, 1).wait_send()
                    elif p < prompt:
                        scatter(p, 1, 0).wait_send()

    def settle_back(role):
        for owner in range(2):
            for i in range(counts[owner]):
                p = static_slot(i, owner)
                owned = role == (0, 3)[owner]
                stops = role == (3, 0)[owner]
                if owned or not is_direct(i, owner):
                    give(p).wait_send()
                if not is_direct(i, owner):
                    given(p).wait_recv()
                if not stops:
                    onward(p, owner, True).wait_send()
                    if is_direct(i, owner):
                        onward(p, owner, False).wait_send()

    def follow(role):
        for event in plan(role, counts):
            kind, owner, i = event
            if kind == "solve":
                solve(i, owner)
            elif kind == "pass":
                pass_other(i, owner)
            elif kind == "down":
                relay_down(i)
            elif kind == "up":
                relay_up(i)
            elif kind == "join":
                join_up(i)
            elif kind == "sums":
                settle_sums(role)
            else:
                accept(i, owner, kind == "own", role == (3, 0)[owner])
        settle_back(role)

    pl.when(first)(lambda: follow(0))
    pl.when(jnp.logical_not(is_end) & (near == 0))(lambda: follow(1))
    pl.when(jnp.logical_not(is_end) & (near == 1))(lambda: follow(2))
    pl.when(final)(lambda: follow(3))


def flush_kernel(block, hold, shifted, out, ring, sem):
    slots = ring.shape[0]
    pairs = out.shape[1] // (2 * LANES)

    def lanes(p):
        return pl.ds(pl.multiple_of(p * (2 * LANES), LANES), 2 * LANES)

    def store(p):
        slot = lax.rem(p, slots)
        return pltpu.make_async_copy(ring.at[slot], out.at[:, lanes(p)], sem.at[slot])

    @pl.loop(0, pairs)
    def _(p):
        @pl.when(p >= slots)
        def _():
            store(p - slots).wait()

        high, low = split(hold[:, lanes(p)])
        both = jnp.dot(shifted[...], jnp.concatenate([high, high], axis=0), preferred_element_type=jnp.float32)
        rest = jnp.dot(shifted[:, :PANEL], low, preferred_element_type=jnp.float32)
        ring[lax.rem(p, slots)] = block[:, lanes(p)] - (both + rest)
        store(p).start()

    @pl.loop(pairs - slots, pairs)
    def _(p):
        store(p).wait()


def flush(block, hold, shifted):
    height, width = block.shape
    vmem = pl.BlockSpec(memory_space=pltpu.VMEM)
    return pl.pallas_call(
        flush_kernel,
        out_shape=jax.ShapeDtypeStruct(block.shape, block.dtype),
        in_specs=[vmem] * 3,
        out_specs=pl.BlockSpec(memory_space=pl.ANY),
        scratch_shapes=[pltpu.VMEM((4, height, 2 * LANES), jnp.float32), pltpu.SemaphoreType.DMA((4,))],
        compiler_params=pltpu.CompilerParams(vmem_limit_bytes=16 * 1024 * 1024),
        name="flush",
    )(block, hold, shifted)


def on_device(n_row, n_col, matrix):
    height, width = matrix.shape
    piece = PANEL // n_row
    blocks = width // (4 * LANES)
    pairs = 2 * blocks
    most = owned_counts(pairs)[0]
    dma = pltpu.SemaphoreType.DMA
    f32, bf16 = jnp.float32, jnp.bfloat16
    parts = pl.pallas_call(
        functools.partial(step_kernel, n_row, n_col),
        out_shape=(
            jax.ShapeDtypeStruct((height, width), f32),
            jax.ShapeDtypeStruct((PANEL, width), f32),
            jax.ShapeDtypeStruct((height, 2 * PANEL), bf16),
        ),
        in_specs=[pl.BlockSpec(memory_space=pl.ANY)],
        out_specs=(pl.BlockSpec(memory_space=pltpu.VMEM),) * 3,
        scratch_shapes=[
            pltpu.VMEM((PANEL, width), f32),
            pltpu.VMEM((pairs, PANEL, LANES), f32),
            pltpu.VMEM((pairs, 2, PANEL, LANES), f32),
            pltpu.VMEM((most, PANEL, LANES), f32),
            pltpu.VMEM((2 * PANEL, height), bf16),
            pltpu.VMEM((height, PANEL), f32),
            pltpu.VMEM((PANEL, PANEL), f32),
            pltpu.VMEM((PANEL, PANEL), f32),
            pltpu.VMEM((PANEL, 2 * PANEL), f32),
            pltpu.VMEM((n_row, piece, PANEL), f32),
            pltpu.VMEM((n_row - 1, piece, PANEL), f32),
            pltpu.VMEM((n_row, piece, PANEL), f32),
            dma((1,)),
            dma((blocks,)),
            dma((most,)),
            dma((n_col,)),
            dma((1,)),
            dma((n_row - 1,)),
            dma((n_row - 1,)),
            dma((4,)),
            dma((n_row,)),
            dma((4,)),
            dma((1,)),
            dma((n_col - 1, 2)),
            dma((2,)),
            dma((pairs, 2)),
            dma((most,)),
            dma((pairs,)),
            dma((pairs,)),
            dma((pairs, 2)),
            dma((pairs, 2)),
            dma((pairs,)),
            dma((pairs,)),
            dma((pairs, 2)),
            dma((pairs, 2)),
        ],
        compiler_params=pltpu.CompilerParams(
            collective_id=0, has_side_effects=True, vmem_limit_bytes=36 * 1024 * 1024
        ),
        name="whole_step",
    )(matrix)
    return flush(*parts)


def solution(mesh):
    body = functools.partial(on_device, mesh.shape["row"], mesh.shape["col"])
    return jax.shard_map(body, mesh=mesh, in_specs=(P("row", "col"),), out_specs=P("row", "col"), check_vma=False)
```

```python
import functools

import jax
import jax.numpy as jnp
from jax import lax
from jax.experimental import pallas as pl
from jax.experimental.pallas import tpu as pltpu
from jax.sharding import PartitionSpec as P

PANEL = 128
STRIP = 8
LANES = 128
MESH = pl.DeviceIdType.MESH
EARLY = 8
LATE = 7
UP_SHARE = 4
LEAD_PACE = 2.5
HOP = 3.5


def dot_exact(a, b, contract):
    return lax.dot_general(
        a, b, (contract, ((), ())), precision=lax.Precision.HIGHEST, preferred_element_type=jnp.float32
    )


def factor_values(gram, top, between=lambda strip: None):
    strips = PANEL // STRIP
    shape = (STRIP, LANES)
    rows = lax.broadcasted_iota(jnp.int32, shape, 0)
    lanes = lax.broadcasted_iota(jnp.int32, shape, 1)
    eye = (
        lax.broadcasted_iota(jnp.int32, (PANEL, PANEL), 0) == lax.broadcasted_iota(jnp.int32, (PANEL, PANEL), 1)
    ).astype(jnp.float32)
    chol = jnp.concatenate([gram, eye], axis=1)
    work = jnp.concatenate([top, jnp.zeros_like(top)], axis=1)
    factor_rows = []
    previous = None

    def spread(x, start):
        return [jnp.broadcast_to(x[:, start + c : start + c + 1], shape) for c in range(STRIP)]

    for strip in range(strips + 1):
        at, back = strip * STRIP, (strip - 1) * STRIP
        if strip < strips:
            between(strip)
            panel = chol[:STRIP]
            columns = spread(panel, at)
            halves = [panel[:, :LANES], panel[:, LANES:]]
            scale = jnp.ones(shape, jnp.float32)
        if strip > 0:
            inner = work[back : back + STRIP] + previous
            aside = work[:, back : back + STRIP]
            inner_columns = spread(inner, back)
            inner_halves = [inner[:, :LANES], inner[:, LANES:]]
        for j in range(STRIP):
            if strip < strips:
                pivot = columns[j][j : j + 1]
                multiplier = jnp.where(rows > j, columns[j] * (1.0 / pivot), 0.0)
                scale = jnp.where(rows == j, lax.rsqrt(pivot), scale)
                columns = [x if c <= j else x - multiplier * x[j : j + 1] for c, x in enumerate(columns)]
                halves = [x - multiplier * x[j : j + 1] for x in halves]
            if strip > 0:
                column = inner_columns[j]
                inverse = 1.0 / column[j : j + 1]

                def eliminate(x):
                    pivot_row = x[j : j + 1] * inverse
                    return jnp.where(rows == j, pivot_row, x - column * pivot_row)

                inner_columns = [x if c <= j else eliminate(x) for c, x in enumerate(inner_columns)]
                inner_halves = [eliminate(x) for x in inner_halves]
        if strip < strips:
            halves = [halves[0] * scale, halves[1] * scale]
            halves[0] = jnp.where(lanes >= at + rows, halves[0], 0.0)
            panel = jnp.concatenate(halves, axis=1)
            factor_rows.append(halves[0])
            if strip < strips - 1:
                chol = chol[STRIP:] - dot_exact(panel[:, at + STRIP : PANEL], panel, ((0,), (0,)))
        if strip > 0:
            inner = jnp.concatenate(inner_halves, axis=1)
            update = dot_exact(aside, inner, ((1,), (0,)))
            pieces = []
            if back > 0:
                pieces.append(work[:back] - update[:back])
            pieces.append(inner)
            if strip < strips:
                pieces.append(work[at:] - update[at:])
            work = jnp.concatenate(pieces, axis=0)
        previous = panel
    return jnp.concatenate(factor_rows, axis=0), work[:, PANEL:]


def send(src, dst, send_sem, recv_sem, target):
    return pltpu.make_async_remote_copy(
        src_ref=src, dst_ref=dst, send_sem=send_sem, recv_sem=recv_sem, device_id=target, device_id_type=MESH
    )


def split(x):
    high = x.astype(jnp.bfloat16)
    return high, (x - high.astype(jnp.float32)).astype(jnp.bfloat16)


def owned_counts(pairs):
    return pairs - pairs // UP_SHARE, pairs // UP_SHARE


def slot_of(i, owner, n_up):
    if owner == 1:
        return 2 * i + 1
    return 2 * i if i < n_up else i + n_up


def is_direct(i, owner):
    return owner == 1


def plan(role, counts, prompt):
    events = []

    def put(time, kind, owner, i):
        events.append((time, len(events), (kind, owner, i)))

    held = [0, 0]
    turns = sorted((slot_of(i, owner, counts[1]), owner, i) for owner in range(2) for i in range(counts[owner]))
    for p, owner, i in turns:
        after = held[owner]
        if p >= prompt:
            held[owner] += 1
            if role == 0:
                put(26.0 + 0.1 * i if owner == 1 else 27.0 + 0.7 * after, "late", owner, i)
        if owner == 0:
            sent = 30.7 + 1.7 * i
            if role == 0:
                put(27.3 + 0.7 * i, "solve", 0, i)
            else:
                put(sent + HOP * role, "own", 0, i)
            if role in (1, 2):
                put(21.2 + 1.4 * i + 3.2 * (2 - role), "down", 0, i)
            continue
        near, away, join, solved = 25.0 + 2.8 * i, 29.0 + 2.8 * i, 33.0 + 2.8 * i, 37.0 + 2.8 * i
        if p >= prompt:
            near, away, join, solved = 34.0 + 3.5 * after, 37.5 + 3.5 * after, 41.0 + 3.5 * after, 46.0 + 3.0 * after
        if role == 3:
            put(solved, "solve", 1, i)
            put(solved + HOP, "pass", 1, i)
        else:
            put(solved + HOP * (3 - role), "own", 1, i)
            put(solved + HOP * (4 - role), "other", 1, i)
        if role == 1:
            put(near, "up", 1, i)
        if role == 2:
            put(away, "up", 1, i)
            put(join, "join", 1, i)
    put(99.0, "sums", 0, 0)
    return [event for _, _, event in sorted(events)]


def step_kernel(
    n_row, n_col, matrix_ref, hold, shifted,
    block, partial, pair_in, chain_in, top_in, stacked, panel, top, factor_ref, inverse_ref,
    parts, arrived, whole,
    fetch_sem, block_sem, own_sem,
    panel_send, panel_recv, part_send, part_recv, whole_send, whole_recv, top_send, top_recv, share_send, share_recv,
    scatter_send, scatter_recv, pair_send, pair_recv, chain_send, chain_recv,
    give_send, give_recv, pass_send, pass_recv,
):
    row, col = lax.axis_index("row"), lax.axis_index("col")
    width = block.shape[1]
    blocks = width // (4 * LANES)
    pairs = 2 * blocks
    counts = owned_counts(pairs)
    prompt = pairs - LATE
    piece = PANEL // n_row
    outer_n = n_row // 2
    last = outer_n - 1
    outer, inner = row // 2, lax.rem(row, 2)
    other = 1 - inner
    partner = {"row": outer * 2 + other}
    first, final = outer == 0, outer == last
    is_end = first | final
    mine = jnp.where(first, 0, 1)
    near = jnp.where(2 * outer < outer_n, 0, 1)
    end_rows = [0, 1, n_row - 2, n_row - 1]

    barrier = pltpu.get_barrier_semaphore()
    for d in range(1, n_row):
        pl.semaphore_signal(barrier, inc=1, device_id={"row": lax.rem(row + d, n_row)}, device_id_type=MESH)
    for d in range(1, n_col):
        pl.semaphore_signal(barrier, inc=1, device_id={"col": lax.rem(col + d, n_col)}, device_id_type=MESH)

    def lanes(start, size):
        return pl.ds(pl.multiple_of(start, LANES), size)

    def unit(p, side):
        return lanes(p * (2 * LANES) + side * LANES, LANES)

    def load(j):
        place = lanes(j * (4 * LANES), 4 * LANES)
        return pltpu.make_async_copy(matrix_ref.at[:, place], block.at[:, place], block_sem.at[j])

    def static_slot(i, owner):
        return slot_of(i, owner, counts[1])

    def owner_of(p):
        return jnp.where((p < 2 * counts[1]) & (lax.rem(p, 2) == 1), 1, 0)

    def turn_of(p):
        return jnp.where(p < 2 * counts[1], lax.div(p, 2), p - counts[1])

    def scatter(p, side, up):
        return send(
            matrix_ref.at[pl.ds(0, PANEL), unit(p, side)], top_in.at[turn_of(p)],
            scatter_send.at[p, side], scatter_recv.at[turn_of(p)], {"row": end_rows[2 * up + side]},
        )

    def keep(i):
        place = unit(static_slot(i, 0), 0)
        return pltpu.make_async_copy(matrix_ref.at[pl.ds(0, PANEL), place], top_in.at[i], own_sem.at[i])

    def start_scatter(p):
        @pl.when((row == 0) & (owner_of(p) == 0) & (p < prompt))
        def _():
            scatter(p, 1, 0).start()

    def start_up(i):
        @pl.when((row == 0) & (static_slot(i, 1) < prompt))
        def _():
            for side in range(2):
                scatter(static_slot(i, 1), side, 1).start()

    def pair(p):
        return send(partial.at[:, unit(p, other)], pair_in.at[p], pair_send.at[p], pair_recv.at[p], partner)

    def chain(p, towards, own):
        slot = 0 if own else 1
        return send(
            partial.at[:, unit(p, inner if own else other)], chain_in.at[p, slot],
            chain_send.at[p, slot], chain_recv.at[p, slot], {"row": row + 2 * (2 * towards - 1)},
        )

    joins = outer == last - 1

    def give(p):
        place = unit(p, inner)
        return send(hold.at[:, place], hold.at[:, place], give_send.at[p], give_recv.at[p], partner)

    def given(p):
        place = unit(p, other)
        return send(hold.at[:, place], hold.at[:, place], give_send.at[p], give_recv.at[p], partner)

    def onward(p, owner, own):
        place = unit(p, inner if own else other)
        slot = 0 if own else 1
        return send(
            hold.at[:, place], hold.at[:, place], pass_send.at[p, slot], pass_recv.at[p, slot],
            {"row": row + 2 * (1 - 2 * owner)},
        )

    def multiply(j):
        place = lanes(j * (4 * LANES), 4 * LANES)
        high, low = split(block[:, place])
        both = jnp.dot(stacked[...], high, preferred_element_type=jnp.float32)
        rest = jnp.dot(stacked[:PANEL], low, preferred_element_type=jnp.float32)
        partial[:, place] = both[:PANEL] + both[PANEL:] + rest

    def exchange(p):
        owner = owner_of(p)

        prompt_here = jnp.logical_not((row == 0) & (p >= prompt))

        @pl.when((owner == 0) & prompt_here)
        def _():
            pair(p).start()

        @pl.when((owner == 1) & first & prompt_here)
        def _():
            chain(p, owner, True).start()
            chain(p, owner, False).start()

    def exchange_last():
        @pl.when(final)
        def _():
            for i in range(counts[1]):
                pair(static_slot(i, 1)).start()

    def prepare():
        high, low = split(panel[...])
        shifted[:, :PANEL] = high
        shifted[:, PANEL:] = low
        high, low = split(jnp.transpose(panel[...]))
        stacked[:PANEL] = high
        stacked[PANEL:] = low

    def multiply_range(start, stop, ahead):
        @pl.loop(start, stop)
        def _(j):
            load(j).wait()
            multiply(j)
            for p in (2 * j, 2 * j + 1):
                exchange(p)

                @pl.when(p + ahead < pairs)
                def _():
                    start_scatter(p + ahead)

    @pl.when(col == 0)
    def _():
        fetch = pltpu.make_async_copy(matrix_ref.at[:, pl.ds(0, PANEL)], panel, fetch_sem.at[0])
        fetch.start()
        fetch.wait()
        for j in range(blocks):
            load(j).start()
        local = dot_exact(panel[...], panel[...], ((0,), (0,)))
        for q in range(n_row):
            parts[q] = local[q * piece : (q + 1) * piece]

    @pl.when(col != 0)
    def _():
        for j in range(blocks):
            load(j).start()

    @pl.when(row == 0)
    def _():
        for i in range(counts[0]):
            if static_slot(i, 0) < prompt:
                keep(i).start()

    pl.semaphore_wait(barrier, n_row - 1 + n_col - 1)

    def panel_copy(to, slot):
        return send(panel, panel, panel_send.at[slot], panel_recv.at[0], {"col": to})

    heads = [1] + [c for c in range(2, n_col, 2)]

    @pl.when(col == 0)
    def _():
        def part(d):
            q = lax.rem(row + d, n_row)
            return send(parts.at[q], arrived.at[d - 1], part_send.at[d - 1], part_recv.at[d - 1], {"row": q})

        def whole_copy(e):
            return send(whole.at[row], whole.at[row], whole_send.at[e], whole_recv.at[row], {"row": end_rows[e]})

        def top_copy(e):
            return send(panel.at[pl.ds(0, PANEL)], top, top_send.at[e], top_recv.at[0], {"row": end_rows[e]})

        def share(c, slot):
            ref = (top, whole)[slot]
            return send(ref, ref, share_send.at[c - 1, slot], share_recv.at[slot], {"col": c})

        for d in range(1, n_row):
            part(d).start()
        for slot, c in enumerate(heads[1:]):
            panel_copy(c, slot + 1).start()

        @pl.when(row == 0)
        def _():
            for e in range(1, 4):
                top_copy(e).start()
            top[...] = panel[:PANEL]

        prepare()

        @pl.loop(0, blocks // 2)
        def _(j):
            load(j).wait()
            multiply(j)

        total = parts[row]
        for d in range(1, n_row):
            part(d).wait_recv()
            total = total + arrived[d - 1]
        whole[row] = total
        for e in range(4):
            @pl.when(row != end_rows[e])
            def _():
                whole_copy(e).start()

        panel_copy(heads[0], 0).start()
        for i in range(counts[1]):
            start_up(i)

        @pl.loop(0, 2 * (blocks // 2))
        def _(p):
            exchange(p)

            start_scatter(p)

        @pl.when(is_end)
        def _():
            @pl.when(row != 0)
            def _():
                send(top, top, top_send.at[0], top_recv.at[0], {"row": 0}).wait_recv()

            for c in range(1, n_col):
                share(c, 0).start()

        multiply_range(blocks // 2, blocks, 0)
        exchange_last()

        @pl.when(is_end)
        def _():
            for q in range(n_row):
                @pl.when(row != q)
                def _():
                    send(whole.at[q], whole.at[q], whole_send.at[0], whole_recv.at[q], {"row": q}).wait_recv()
            for c in range(1, n_col):
                share(c, 1).start()
            for c in range(1, n_col):
                share(c, 0).wait_send()
                share(c, 1).wait_send()

        for d in range(1, n_row):
            part(d).wait_send()
        for slot, c in enumerate(heads):
            panel_copy(c, slot).wait_send()
        for e in range(4):
            @pl.when(row != end_rows[e])
            def _():
                whole_copy(e).wait_send()

        @pl.when(row == 0)
        def _():
            for e in range(1, 4):
                top_copy(e).wait_send()

    @pl.when(col != 0)
    def _():
        @pl.when(col != 1)
        def _():
            for p in range(EARLY):
                start_scatter(p)
            for i in range(counts[1]):
                start_up(i)

        root = {"col": 0}
        send(panel, panel, panel_send.at[0], panel_recv.at[0], root).wait_recv()
        relay = (lax.rem(col, 2) == 0) & (col + 1 < n_col)

        @pl.when(relay)
        def _():
            panel_copy(col + 1, 0).start()

        @pl.when(col == 1)
        def _():
            for i in range(counts[1]):
                start_up(i)

        prepare()
        ahead = jnp.where(col == 1, 0, EARLY)
        multiply_range(0, blocks, ahead)
        exchange_last()

        @pl.when(is_end)
        def _():
            send(top, top, share_send.at[0, 0], share_recv.at[0], root).wait_recv()
            send(whole, whole, share_send.at[0, 1], share_recv.at[1], root).wait_recv()

        @pl.when(relay)
        def _():
            panel_copy(col + 1, 0).wait_send()

    def add(p, side, *terms):
        place = unit(p, side)
        total = partial[:, place]
        for term in terms:
            total = total + term[...]
        partial[:, place] = total

    def lead(i):
        p = static_slot(i, 0)
        pair(p).wait_recv()
        add(p, inner, pair_in.at[p])
        chain(p, 0, True).start()

    def relay_down(i):
        p = static_slot(i, 0)
        pair(p).wait_recv()
        chain(p, 0, True).wait_recv()
        add(p, inner, pair_in.at[p], chain_in.at[p, 0])
        chain(p, 0, True).start()

    def relay_up(i):
        p = static_slot(i, 1)
        for own in (False, True):
            chain(p, 1, own).wait_recv()
            add(p, inner if own else other, chain_in.at[p, 0 if own else 1])

            @pl.when(jnp.logical_not(joins))
            def _():
                chain(p, 1, own).start()

            if not own:
                @pl.when(joins)
                def _():
                    pair(p).start()

    def join_up(i):
        @pl.when(joins)
        def _():
            p = static_slot(i, 1)
            pair(p).wait_recv()
            add(p, inner, pair_in.at[p])
            chain(p, 1, True).start()

    @pl.when(is_end)
    def _():
        gram = jnp.concatenate([whole[q] for q in range(n_row)], axis=0)

        strips = [2 + int(LEAD_PACE * i) for i in range(counts[0])]

        def between(strip):
            if strip in strips:
                @pl.when(final)
                def _():
                    lead(strips.index(strip))

        factor, inverse = factor_values(gram, top[...], between)
        factor_ref[...] = factor
        inverse_ref[:, :PANEL] = inverse
        inverse_ref[:, PANEL:] = dot_exact(inverse, factor, ((1,), (1,)))

        @pl.when(final)
        def _():
            for i in range(counts[0]):
                if strips[i] >= PANEL // STRIP:
                    lead(i)

        @pl.when(row == 0)
        def _():
            high, low = split(panel[:PANEL] + factor)
            shifted[:PANEL, :PANEL] = high
            shifted[:PANEL, PANEL:] = low

    def late(i, owner):
        p = static_slot(i, owner)

        @pl.when(row == 0)
        def _():
            place = unit(p, 1) if owner == 0 else lanes(p * (2 * LANES), 2 * LANES)
            extra = dot_exact(factor_ref[...], block[:PANEL, place], ((0,), (0,)))
            partial[:, place] = partial[:, place] + extra
            if owner == 0:
                pair(p).start()
            else:
                chain(p, 1, True).start()
                chain(p, 1, False).start()

    def solve(i, owner):
        p = static_slot(i, owner)
        pair(p).wait_recv()
        chain(p, owner, True).wait_recv()
        place = unit(p, inner)
        held = p >= prompt

        def at_row_zero():
            if held:
                top_in[i] = block[:PANEL, place]
            else:
                keep(i).wait()

        def elsewhere():
            if held:
                top_in[i] = jnp.zeros((PANEL, LANES), jnp.float32)
            else:
                send(top_in.at[i], top_in.at[i], scatter_send.at[0, 0], scatter_recv.at[i], {"row": 0}).wait_recv()

        if owner == 0:
            pl.when(row == 0)(at_row_zero)
            pl.when(row != 0)(elsewhere)
        else:
            elsewhere()
        total = partial[:, place] + pair_in[p] + chain_in[p, 0]
        hold[:, place] = dot_exact(inverse_ref[...], jnp.concatenate([total, top_in[i]], axis=0), ((1,), (0,)))
        onward(p, owner, True).start()
        give(p).start()

    def pass_other(i, owner):
        p = static_slot(i, owner)
        given(p).wait_recv()
        onward(p, owner, False).start()

    def accept(i, owner, own, stops):
        p = static_slot(i, owner)
        onward(p, owner, own).wait_recv()
        if not stops:
            onward(p, owner, own).start()
        if own and not is_direct(i, owner):
            give(p).start()

    turns = sorted((static_slot(i, owner), owner, i) for owner in range(2) for i in range(counts[owner]))

    def settle_sums(role):
        for p, owner, _ in turns:
            if owner == 0:
                pair(p).wait_send()
                if role != 0:
                    chain(p, 0, True).wait_send()
            elif role == 0:
                chain(p, 1, True).wait_send()
                chain(p, 1, False).wait_send()
            elif role == 3:
                pair(p).wait_send()
            else:
                chain(p, 1, True).wait_send()

                @pl.when(joins)
                def _():
                    pair(p).wait_send()

                @pl.when(jnp.logical_not(joins))
                def _():
                    chain(p, 1, False).wait_send()
        if role == 0:
            @pl.when(row == 0)
            def _():
                for p, owner, _ in turns:
                    if owner == 1 and p < prompt:
                        scatter(p, 0, 1).wait_send()
                        scatter(p, 1, 1).wait_send()
                    elif p < prompt:
                        scatter(p, 1, 0).wait_send()

    def settle_back(role):
        for owner in range(2):
            for i in range(counts[owner]):
                p = static_slot(i, owner)
                owned = role == (0, 3)[owner]
                stops = role == (3, 0)[owner]
                if owned or not is_direct(i, owner):
                    give(p).wait_send()
                if not is_direct(i, owner):
                    given(p).wait_recv()
                if not stops:
                    onward(p, owner, True).wait_send()
                    if is_direct(i, owner):
                        onward(p, owner, False).wait_send()

    def follow(role):
        for event in plan(role, counts, prompt):
            kind, owner, i = event
            if kind == "solve":
                solve(i, owner)
            elif kind == "late":
                late(i, owner)
            elif kind == "pass":
                pass_other(i, owner)
            elif kind == "down":
                relay_down(i)
            elif kind == "up":
                relay_up(i)
            elif kind == "join":
                join_up(i)
            elif kind == "sums":
                settle_sums(role)
            else:
                accept(i, owner, kind == "own", role == (3, 0)[owner])
        settle_back(role)

    pl.when(first)(lambda: follow(0))
    pl.when(jnp.logical_not(is_end) & (near == 0))(lambda: follow(1))
    pl.when(jnp.logical_not(is_end) & (near == 1))(lambda: follow(2))
    pl.when(final)(lambda: follow(3))


def flush_kernel(block, hold, shifted, out, ring, sem):
    slots = ring.shape[0]
    pairs = out.shape[1] // (2 * LANES)

    def lanes(p):
        return pl.ds(pl.multiple_of(p * (2 * LANES), LANES), 2 * LANES)

    def store(p):
        slot = lax.rem(p, slots)
        return pltpu.make_async_copy(ring.at[slot], out.at[:, lanes(p)], sem.at[slot])

    @pl.loop(0, pairs)
    def _(p):
        @pl.when(p >= slots)
        def _():
            store(p - slots).wait()

        high, low = split(hold[:, lanes(p)])
        both = jnp.dot(shifted[...], jnp.concatenate([high, high], axis=0), preferred_element_type=jnp.float32)
        rest = jnp.dot(shifted[:, :PANEL], low, preferred_element_type=jnp.float32)
        ring[lax.rem(p, slots)] = block[:, lanes(p)] - (both + rest)
        store(p).start()

    @pl.loop(pairs - slots, pairs)
    def _(p):
        store(p).wait()


def flush(block, hold, shifted):
    height, width = block.shape
    vmem = pl.BlockSpec(memory_space=pltpu.VMEM)
    return pl.pallas_call(
        flush_kernel,
        out_shape=jax.ShapeDtypeStruct(block.shape, block.dtype),
        in_specs=[vmem] * 3,
        out_specs=pl.BlockSpec(memory_space=pl.ANY),
        scratch_shapes=[pltpu.VMEM((4, height, 2 * LANES), jnp.float32), pltpu.SemaphoreType.DMA((4,))],
        compiler_params=pltpu.CompilerParams(vmem_limit_bytes=16 * 1024 * 1024),
        name="flush",
    )(block, hold, shifted)


def on_device(n_row, n_col, matrix):
    height, width = matrix.shape
    piece = PANEL // n_row
    blocks = width // (4 * LANES)
    pairs = 2 * blocks
    most = owned_counts(pairs)[0]
    dma = pltpu.SemaphoreType.DMA
    f32, bf16 = jnp.float32, jnp.bfloat16
    hold, shifted = pl.pallas_call(
        functools.partial(step_kernel, n_row, n_col),
        out_shape=(
            jax.ShapeDtypeStruct((PANEL, width), f32),
            jax.ShapeDtypeStruct((height, 2 * PANEL), bf16),
        ),
        in_specs=[pl.BlockSpec(memory_space=pltpu.HBM)],
        out_specs=(pl.BlockSpec(memory_space=pltpu.VMEM),) * 2,
        scratch_shapes=[
            pltpu.VMEM((height, width), f32),
            pltpu.VMEM((PANEL, width), f32),
            pltpu.VMEM((pairs, PANEL, LANES), f32),
            pltpu.VMEM((pairs, 2, PANEL, LANES), f32),
            pltpu.VMEM((most, PANEL, LANES), f32),
            pltpu.VMEM((2 * PANEL, height), bf16),
            pltpu.VMEM((height, PANEL), f32),
            pltpu.VMEM((PANEL, PANEL), f32),
            pltpu.VMEM((PANEL, PANEL), f32),
            pltpu.VMEM((PANEL, 2 * PANEL), f32),
            pltpu.VMEM((n_row, piece, PANEL), f32),
            pltpu.VMEM((n_row - 1, piece, PANEL), f32),
            pltpu.VMEM((n_row, piece, PANEL), f32),
            dma((1,)),
            dma((blocks,)),
            dma((most,)),
            dma((n_col,)),
            dma((1,)),
            dma((n_row - 1,)),
            dma((n_row - 1,)),
            dma((4,)),
            dma((n_row,)),
            dma((4,)),
            dma((1,)),
            dma((n_col - 1, 2)),
            dma((2,)),
            dma((pairs, 2)),
            dma((most,)),
            dma((pairs,)),
            dma((pairs,)),
            dma((pairs, 2)),
            dma((pairs, 2)),
            dma((pairs,)),
            dma((pairs,)),
            dma((pairs, 2)),
            dma((pairs, 2)),
        ],
        compiler_params=pltpu.CompilerParams(
            collective_id=0, has_side_effects=True, vmem_limit_bytes=44 * 1024 * 1024
        ),
        name="whole_step",
    )(matrix)
    return flush(matrix, hold, shifted)


def solution(mesh):
    body = functools.partial(on_device, mesh.shape["row"], mesh.shape["col"])
    return jax.shard_map(body, mesh=mesh, in_specs=(P("row", "col"),), out_specs=P("row", "col"), check_vma=False)
```

```python
import functools

import jax
import jax.numpy as jnp
from jax import lax
from jax.experimental import pallas as pl
from jax.experimental.pallas import tpu as pltpu
from jax.sharding import PartitionSpec as P

PANEL = 128
STRIP = 8
LANES = 128
MESH = pl.DeviceIdType.MESH
EARLY = 8
LATE = 7
UP_SHARE = 4
LEAD_PACE = 2.5
HOP = 4.1


def dot_exact(a, b, contract):
    return lax.dot_general(
        a, b, (contract, ((), ())), precision=lax.Precision.HIGHEST, preferred_element_type=jnp.float32
    )


def factor_values(gram, top, between=lambda strip: None):
    strips = PANEL // STRIP
    shape = (STRIP, LANES)
    rows = lax.broadcasted_iota(jnp.int32, shape, 0)
    lanes = lax.broadcasted_iota(jnp.int32, shape, 1)
    eye = (
        lax.broadcasted_iota(jnp.int32, (PANEL, PANEL), 0) == lax.broadcasted_iota(jnp.int32, (PANEL, PANEL), 1)
    ).astype(jnp.float32)
    chol = jnp.concatenate([gram, eye], axis=1)
    work = jnp.concatenate([top, jnp.zeros_like(top)], axis=1)
    factor_rows = []
    previous = None

    def spread(x, start):
        return [jnp.broadcast_to(x[:, start + c : start + c + 1], shape) for c in range(STRIP)]

    for strip in range(strips + 1):
        at, back = strip * STRIP, (strip - 1) * STRIP
        if strip < strips:
            between(strip)
            panel = chol[:STRIP]
            columns = spread(panel, at)
            halves = [panel[:, :LANES], panel[:, LANES:]]
            scale = jnp.ones(shape, jnp.float32)
        if strip > 0:
            inner = work[back : back + STRIP] + previous
            aside = work[:, back : back + STRIP]
            inner_columns = spread(inner, back)
            inner_halves = [inner[:, :LANES], inner[:, LANES:]]
        for j in range(STRIP):
            if strip < strips:
                pivot = columns[j][j : j + 1]
                multiplier = jnp.where(rows > j, columns[j] * (1.0 / pivot), 0.0)
                scale = jnp.where(rows == j, lax.rsqrt(pivot), scale)
                columns = [x if c <= j else x - multiplier * x[j : j + 1] for c, x in enumerate(columns)]
                halves = [x - multiplier * x[j : j + 1] for x in halves]
            if strip > 0:
                column = inner_columns[j]
                inverse = 1.0 / column[j : j + 1]

                def eliminate(x):
                    pivot_row = x[j : j + 1] * inverse
                    return jnp.where(rows == j, pivot_row, x - column * pivot_row)

                inner_columns = [x if c <= j else eliminate(x) for c, x in enumerate(inner_columns)]
                inner_halves = [eliminate(x) for x in inner_halves]
        if strip < strips:
            halves = [halves[0] * scale, halves[1] * scale]
            halves[0] = jnp.where(lanes >= at + rows, halves[0], 0.0)
            panel = jnp.concatenate(halves, axis=1)
            factor_rows.append(halves[0])
            if strip < strips - 1:
                chol = chol[STRIP:] - dot_exact(panel[:, at + STRIP : PANEL], panel, ((0,), (0,)))
        if strip > 0:
            inner = jnp.concatenate(inner_halves, axis=1)
            update = dot_exact(aside, inner, ((1,), (0,)))
            pieces = []
            if back > 0:
                pieces.append(work[:back] - update[:back])
            pieces.append(inner)
            if strip < strips:
                pieces.append(work[at:] - update[at:])
            work = jnp.concatenate(pieces, axis=0)
        previous = panel
    return jnp.concatenate(factor_rows, axis=0), work[:, PANEL:]


def send(src, dst, send_sem, recv_sem, target):
    return pltpu.make_async_remote_copy(
        src_ref=src, dst_ref=dst, send_sem=send_sem, recv_sem=recv_sem, device_id=target, device_id_type=MESH
    )


def split(x):
    high = x.astype(jnp.bfloat16)
    return high, (x - high.astype(jnp.float32)).astype(jnp.bfloat16)


def owned_counts(pairs):
    return pairs - pairs // UP_SHARE, pairs // UP_SHARE


def slot_of(i, owner, n_up):
    if owner == 1:
        return 2 * i + 1
    return 2 * i if i < n_up else i + n_up


def is_direct(i, owner):
    return owner == 1


def plan(role, counts, prompt):
    events = []

    def put(time, kind, owner, i):
        events.append((time, len(events), (kind, owner, i)))

    held = [0, 0]
    turns = sorted((slot_of(i, owner, counts[1]), owner, i) for owner in range(2) for i in range(counts[owner]))
    for p, owner, i in turns:
        after = held[owner]
        if p >= prompt:
            held[owner] += 1
            if role == 0:
                put(26.0 + 0.1 * i if owner == 1 else 27.0 + 0.7 * after, "late", owner, i)
        if owner == 0:
            sent = 31.4 + 1.5 * i
            if role == 0:
                put(27.3 + 0.7 * i, "solve", 0, i)
            else:
                put(sent + HOP * role, "own", 0, i)
            if role in (1, 2):
                put(21.2 + 1.4 * i + 3.2 * (2 - role), "down", 0, i)
            continue
        near, away, join, solved = 25.0 + 2.8 * i, 29.0 + 2.8 * i, 33.0 + 2.8 * i, 37.0 + 2.4 * i
        if p >= prompt:
            near, away, join, solved = 34.0 + 3.5 * after, 37.5 + 3.5 * after, 41.0 + 3.5 * after, 46.0 + 3.0 * after
        if role == 3:
            put(solved, "solve", 1, i)
            put(solved + 4.5, "pass", 1, i)
        else:
            put(solved + 1.5 + HOP * (3 - role), "own", 1, i)
            put(solved + 2.0 + HOP * (4 - role), "other", 1, i)
        if role == 1:
            put(near, "up", 1, i)
        if role == 2:
            put(away, "up", 1, i)
            put(join, "join", 1, i)
    return [event for _, _, event in sorted(events)]


def step_kernel(
    n_row, n_col, matrix_ref, hold, shifted,
    block, partial, pair_in, chain_in, top_in, stacked, panel, top, factor_ref, inverse_ref,
    parts, arrived, whole,
    fetch_sem, block_sem, own_sem,
    panel_send, panel_recv, part_send, part_recv, whole_send, whole_recv, top_send, top_recv, share_send, share_recv,
    scatter_send, scatter_recv, pair_send, pair_recv, chain_send, chain_recv,
    give_send, give_recv, pass_send, pass_recv,
):
    row, col = lax.axis_index("row"), lax.axis_index("col")
    width = block.shape[1]
    blocks = width // (4 * LANES)
    pairs = 2 * blocks
    counts = owned_counts(pairs)
    prompt = pairs - LATE
    piece = PANEL // n_row
    outer_n = n_row // 2
    last = outer_n - 1
    outer, inner = row // 2, lax.rem(row, 2)
    other = 1 - inner
    partner = {"row": outer * 2 + other}
    first, final = outer == 0, outer == last
    is_end = first | final
    mine = jnp.where(first, 0, 1)
    near = jnp.where(2 * outer < outer_n, 0, 1)
    end_rows = [0, 1, n_row - 2, n_row - 1]

    barrier = pltpu.get_barrier_semaphore()
    for d in range(1, n_row):
        pl.semaphore_signal(barrier, inc=1, device_id={"row": lax.rem(row + d, n_row)}, device_id_type=MESH)
    for d in range(1, n_col):
        pl.semaphore_signal(barrier, inc=1, device_id={"col": lax.rem(col + d, n_col)}, device_id_type=MESH)

    def lanes(start, size):
        return pl.ds(pl.multiple_of(start, LANES), size)

    def unit(p, side):
        return lanes(p * (2 * LANES) + side * LANES, LANES)

    def load(j):
        place = lanes(j * (4 * LANES), 4 * LANES)
        return pltpu.make_async_copy(matrix_ref.at[:, place], block.at[:, place], block_sem.at[j])

    def static_slot(i, owner):
        return slot_of(i, owner, counts[1])

    def owner_of(p):
        return jnp.where((p < 2 * counts[1]) & (lax.rem(p, 2) == 1), 1, 0)

    def turn_of(p):
        if isinstance(p, int):
            return p // 2 if p < 2 * counts[1] else p - counts[1]
        return jnp.where(p < 2 * counts[1], lax.div(p, 2), p - counts[1])

    def scatter(p, side, up):
        return send(
            matrix_ref.at[pl.ds(0, PANEL), unit(p, side)], top_in.at[turn_of(p)],
            scatter_send.at[0], scatter_recv.at[turn_of(p)], {"row": end_rows[2 * up + side]},
        )

    def keep(i):
        place = unit(static_slot(i, 0), 0)
        return pltpu.make_async_copy(matrix_ref.at[pl.ds(0, PANEL), place], top_in.at[i], own_sem.at[0])

    def start_scatter(p):
        @pl.when((row == 0) & (owner_of(p) == 0) & (p < prompt))
        def _():
            scatter(p, 1, 0).start()

    def start_up(i):
        @pl.when((row == 0) & (static_slot(i, 1) < prompt))
        def _():
            for side in range(2):
                scatter(static_slot(i, 1), side, 1).start()

    def pair(p):
        return send(partial.at[:, unit(p, other)], pair_in.at[p], pair_send.at[0], pair_recv.at[p], partner)

    def chain(p, towards, own):
        slot = way(p, own)
        return send(
            partial.at[:, unit(p, inner if own else other)], chain_in.at[slot],
            chain_send.at[0], chain_recv.at[slot], {"row": row + 2 * (2 * towards - 1)},
        )

    def way(p, own):
        return p if own else pairs + turn_of(p)

    joins = outer == last - 1

    def give(p):
        place = unit(p, inner)
        return send(hold.at[:, place], hold.at[:, place], give_send.at[0], give_recv.at[p], partner)

    def given(p):
        place = unit(p, other)
        return send(hold.at[:, place], hold.at[:, place], give_send.at[0], give_recv.at[p], partner)

    def onward(p, owner, own):
        place = unit(p, inner if own else other)
        slot = way(p, own)
        return send(
            hold.at[:, place], hold.at[:, place], pass_send.at[0], pass_recv.at[slot],
            {"row": row + 2 * (1 - 2 * owner)},
        )

    def multiply(j):
        place = lanes(j * (4 * LANES), 4 * LANES)
        high, low = split(block[:, place])
        both = jnp.dot(stacked[...], high, preferred_element_type=jnp.float32)
        rest = jnp.dot(stacked[:PANEL], low, preferred_element_type=jnp.float32)
        partial[:, place] = both[:PANEL] + both[PANEL:] + rest

    def exchange(p):
        owner = owner_of(p)

        prompt_here = jnp.logical_not((row == 0) & (p >= prompt))

        @pl.when((owner == 0) & prompt_here)
        def _():
            pair(p).start()

        @pl.when((owner == 1) & first & prompt_here)
        def _():
            chain(p, owner, True).start()
            chain(p, owner, False).start()

    def exchange_last():
        @pl.when(final)
        def _():
            for i in range(counts[1]):
                pair(static_slot(i, 1)).start()

    def prepare():
        high, low = split(panel[...])
        shifted[:, :PANEL] = high
        shifted[:, PANEL:] = low
        high, low = split(jnp.transpose(panel[...]))
        stacked[:PANEL] = high
        stacked[PANEL:] = low

    def multiply_range(start, stop, ahead):
        @pl.loop(start, stop)
        def _(j):
            load(j).wait()
            multiply(j)
            for p in (2 * j, 2 * j + 1):
                exchange(p)

                @pl.when(p + ahead < pairs)
                def _():
                    start_scatter(p + ahead)

    @pl.when(col == 0)
    def _():
        fetch = pltpu.make_async_copy(matrix_ref.at[:, pl.ds(0, PANEL)], panel, fetch_sem.at[0])
        fetch.start()
        fetch.wait()
        for j in range(blocks):
            load(j).start()
        local = dot_exact(panel[...], panel[...], ((0,), (0,)))
        for q in range(n_row):
            parts[q] = local[q * piece : (q + 1) * piece]

    @pl.when(col != 0)
    def _():
        for j in range(blocks):
            load(j).start()

    @pl.when(row == 0)
    def _():
        for i in range(counts[0]):
            if static_slot(i, 0) < prompt:
                keep(i).start()

    pl.semaphore_wait(barrier, n_row - 1 + n_col - 1)

    def panel_copy(to, slot):
        return send(panel, panel, panel_send.at[slot], panel_recv.at[0], {"col": to})

    heads = [1] + [c for c in range(2, n_col, 2)]

    @pl.when(col == 0)
    def _():
        def part(d):
            q = lax.rem(row + d, n_row)
            return send(parts.at[q], arrived.at[d - 1], part_send.at[0], part_recv.at[0], {"row": q})

        def whole_copy(e):
            return send(whole.at[row], whole.at[row], whole_send.at[0], whole_recv.at[0], {"row": end_rows[e]})

        def top_copy(e):
            return send(panel.at[pl.ds(0, PANEL)], top, top_send.at[0], top_recv.at[0], {"row": end_rows[e]})

        def share(c, slot):
            ref = (top, whole)[slot]
            return send(ref, ref, share_send.at[0], share_recv.at[slot], {"col": c})

        for d in range(1, n_row):
            part(d).start()
        for slot, c in enumerate(heads[1:]):
            panel_copy(c, slot + 1).start()

        @pl.when(row == 0)
        def _():
            for e in range(1, 4):
                top_copy(e).start()
            top[...] = panel[:PANEL]

        prepare()

        @pl.loop(0, blocks // 2)
        def _(j):
            load(j).wait()
            multiply(j)

        send(arrived, arrived, part_send.at[0], part_recv.at[0], {"row": 0}).wait_recv()
        total = parts[row]
        for d in range(1, n_row):
            total = total + arrived[d - 1]
        whole[row] = total
        for e in range(4):
            @pl.when(row != end_rows[e])
            def _():
                whole_copy(e).start()

        panel_copy(heads[0], 0).start()
        for i in range(counts[1]):
            start_up(i)

        @pl.loop(0, 2 * (blocks // 2))
        def _(p):
            exchange(p)

            start_scatter(p)

        @pl.when(is_end)
        def _():
            @pl.when(row != 0)
            def _():
                send(top, top, top_send.at[0], top_recv.at[0], {"row": 0}).wait_recv()

            for c in range(1, n_col):
                share(c, 0).start()

        multiply_range(blocks // 2, blocks, 0)
        exchange_last()

        @pl.when(is_end)
        def _():
            most = whole.at[pl.ds(0, n_row - 1)]
            send(most, most, whole_send.at[0], whole_recv.at[0], {"row": 0}).wait_recv()
            for c in range(1, n_col):
                share(c, 1).start()

    @pl.when(col != 0)
    def _():
        @pl.when(col != 1)
        def _():
            for p in range(EARLY):
                start_scatter(p)
            for i in range(counts[1]):
                start_up(i)

        root = {"col": 0}
        send(panel, panel, panel_send.at[0], panel_recv.at[0], root).wait_recv()
        relay = (lax.rem(col, 2) == 0) & (col + 1 < n_col)

        @pl.when(relay)
        def _():
            panel_copy(col + 1, 0).start()

        @pl.when(col == 1)
        def _():
            for i in range(counts[1]):
                start_up(i)

        prepare()
        ahead = jnp.where(col == 1, 0, EARLY)
        multiply_range(0, blocks, ahead)
        exchange_last()

        @pl.when(is_end)
        def _():
            send(top, top, share_send.at[0], share_recv.at[0], root).wait_recv()
            send(whole, whole, share_send.at[0], share_recv.at[1], root).wait_recv()

        @pl.when(relay)
        def _():
            panel_copy(col + 1, 0).wait_send()

    def add(p, side, *terms):
        place = unit(p, side)
        total = partial[:, place]
        for term in terms:
            total = total + term[...]
        partial[:, place] = total

    def lead(i):
        p = static_slot(i, 0)
        pair(p).wait_recv()
        add(p, inner, pair_in.at[p])
        chain(p, 0, True).start()

    def relay_down(i):
        p = static_slot(i, 0)
        pair(p).wait_recv()
        chain(p, 0, True).wait_recv()
        add(p, inner, pair_in.at[p], chain_in.at[p])
        chain(p, 0, True).start()

    def relay_up(i):
        p = static_slot(i, 1)
        for own in (False, True):
            chain(p, 1, own).wait_recv()
            add(p, inner if own else other, chain_in.at[way(p, own)])

            @pl.when(jnp.logical_not(joins))
            def _():
                chain(p, 1, own).start()

            if not own:
                @pl.when(joins)
                def _():
                    pair(p).start()

    def join_up(i):
        @pl.when(joins)
        def _():
            p = static_slot(i, 1)
            pair(p).wait_recv()
            add(p, inner, pair_in.at[p])
            chain(p, 1, True).start()

    @pl.when(is_end)
    def _():
        gram = jnp.concatenate([whole[q] for q in range(n_row)], axis=0)

        strips = [2 + int(LEAD_PACE * i) for i in range(counts[0])]

        def between(strip):
            if strip in strips:
                @pl.when(final)
                def _():
                    lead(strips.index(strip))

        factor, inverse = factor_values(gram, top[...], between)
        factor_ref[...] = factor
        inverse_ref[:, :PANEL] = inverse
        inverse_ref[:, PANEL:] = dot_exact(inverse, factor, ((1,), (1,)))

        @pl.when(final)
        def _():
            for i in range(counts[0]):
                if strips[i] >= PANEL // STRIP:
                    lead(i)

        @pl.when(row == 0)
        def _():
            high, low = split(panel[:PANEL] + factor)
            shifted[:PANEL, :PANEL] = high
            shifted[:PANEL, PANEL:] = low

    def late(i, owner):
        p = static_slot(i, owner)

        @pl.when(row == 0)
        def _():
            place = unit(p, 1) if owner == 0 else lanes(p * (2 * LANES), 2 * LANES)
            extra = dot_exact(factor_ref[...], block[:PANEL, place], ((0,), (0,)))
            partial[:, place] = partial[:, place] + extra
            if owner == 0:
                pair(p).start()
            else:
                chain(p, 1, True).start()
                chain(p, 1, False).start()

    def solve(i, owner):
        p = static_slot(i, owner)
        pair(p).wait_recv()
        chain(p, owner, True).wait_recv()
        place = unit(p, inner)
        held = p >= prompt

        def at_row_zero():
            if held:
                top_in[i] = block[:PANEL, place]

        def elsewhere():
            if held:
                top_in[i] = jnp.zeros((PANEL, LANES), jnp.float32)
            else:
                send(top_in.at[i], top_in.at[i], scatter_send.at[0], scatter_recv.at[i], {"row": 0}).wait_recv()

        if owner == 0:
            pl.when(row == 0)(at_row_zero)
            pl.when(row != 0)(elsewhere)
        else:
            elsewhere()
        total = partial[:, place] + pair_in[p] + chain_in[p]
        hold[:, place] = dot_exact(inverse_ref[...], jnp.concatenate([total, top_in[i]], axis=0), ((1,), (0,)))
        onward(p, owner, True).start()
        give(p).start()

    def pass_other(i, owner):
        p = static_slot(i, owner)
        given(p).wait_recv()
        onward(p, owner, False).start()

    def accept(i, owner, own, stops):
        p = static_slot(i, owner)
        onward(p, owner, own).wait_recv()
        if not stops:
            onward(p, owner, own).start()
        if own and not is_direct(i, owner):
            give(p).start()

    turns = sorted((static_slot(i, owner), owner, i) for owner in range(2) for i in range(counts[owner]))

    def drain(sem, units):
        ref = partial.at[:, pl.ds(0, units * LANES)]
        send(ref, ref, sem.at[0], pair_recv.at[0], partner).wait_send()

    downs, ups = counts
    prompt_downs = sum(1 for p, owner, _ in turns if owner == 0 and p < prompt)
    prompt_ups = sum(1 for p, owner, _ in turns if owner == 1 and p < prompt)

    def settle(role):
        for p, owner, i in turns:
            if not is_direct(i, owner):
                given(p).wait_recv()
        drain(give_send, downs + (ups if role == 3 else 0))
        drain(pass_send, (downs, downs + 2 * ups, downs + 2 * ups, 2 * ups)[role])
        if role == 2:
            @pl.when(joins)
            def _():
                drain(pair_send, downs + ups)
                drain(chain_send, downs + ups)

            @pl.when(jnp.logical_not(joins))
            def _():
                drain(pair_send, downs)
                drain(chain_send, downs + 2 * ups)
        else:
            drain(pair_send, downs + (ups if role == 3 else 0))
            drain(chain_send, (2 * ups, downs + 2 * ups, 0, downs)[role])
        if role == 0:
            @pl.when(row == 0)
            def _():
                drain(scatter_send, prompt_downs + 2 * prompt_ups)

        @pl.when(col == 0)
        def _():
            for slot, c in enumerate(heads):
                panel_copy(c, slot).wait_send()
            send(arrived, arrived, part_send.at[0], part_recv.at[0], {"row": 0}).wait_send()
            sent = whole.at[pl.ds(0, 3 if role in (0, 3) else 4)]
            send(sent, sent, whole_send.at[0], whole_recv.at[0], {"row": 0}).wait_send()
            if role in (0, 3):
                drain(share_send, 2 * (n_col - 1))
            if role == 0:
                @pl.when(row == 0)
                def _():
                    drain(top_send, 3)

    def follow(role):
        if role == 0:
            @pl.when(row == 0)
            def _():
                kept = top_in.at[pl.ds(0, prompt_downs)]
                pltpu.make_async_copy(kept, kept, own_sem.at[0]).wait()

        for event in plan(role, counts, prompt):
            kind, owner, i = event
            if kind == "solve":
                solve(i, owner)
            elif kind == "late":
                late(i, owner)
            elif kind == "pass":
                pass_other(i, owner)
            elif kind == "down":
                relay_down(i)
            elif kind == "up":
                relay_up(i)
            elif kind == "join":
                join_up(i)
            else:
                accept(i, owner, kind == "own", role == (3, 0)[owner])
        settle(role)

    pl.when(first)(lambda: follow(0))
    pl.when(jnp.logical_not(is_end) & (near == 0))(lambda: follow(1))
    pl.when(jnp.logical_not(is_end) & (near == 1))(lambda: follow(2))
    pl.when(final)(lambda: follow(3))


def flush_kernel(block, hold, shifted, out, ring, sem):
    slots = ring.shape[0]
    pairs = out.shape[1] // (2 * LANES)

    def lanes(p):
        return pl.ds(pl.multiple_of(p * (2 * LANES), LANES), 2 * LANES)

    def store(p):
        slot = lax.rem(p, slots)
        return pltpu.make_async_copy(ring.at[slot], out.at[:, lanes(p)], sem.at[slot])

    @pl.loop(0, pairs)
    def _(p):
        @pl.when(p >= slots)
        def _():
            store(p - slots).wait()

        high, low = split(hold[:, lanes(p)])
        both = jnp.dot(shifted[...], jnp.concatenate([high, high], axis=0), preferred_element_type=jnp.float32)
        rest = jnp.dot(shifted[:, :PANEL], low, preferred_element_type=jnp.float32)
        ring[lax.rem(p, slots)] = block[:, lanes(p)] - (both + rest)
        store(p).start()

    @pl.loop(pairs - slots, pairs)
    def _(p):
        store(p).wait()


def flush(block, hold, shifted):
    height, width = block.shape
    vmem = pl.BlockSpec(memory_space=pltpu.VMEM)
    return pl.pallas_call(
        flush_kernel,
        out_shape=jax.ShapeDtypeStruct(block.shape, block.dtype),
        in_specs=[vmem] * 3,
        out_specs=pl.BlockSpec(memory_space=pl.ANY),
        scratch_shapes=[pltpu.VMEM((4, height, 2 * LANES), jnp.float32), pltpu.SemaphoreType.DMA((4,))],
        compiler_params=pltpu.CompilerParams(vmem_limit_bytes=16 * 1024 * 1024),
        name="flush",
    )(block, hold, shifted)


def on_device(n_row, n_col, matrix):
    height, width = matrix.shape
    piece = PANEL // n_row
    blocks = width // (4 * LANES)
    pairs = 2 * blocks
    most, ups = owned_counts(pairs)
    dma = pltpu.SemaphoreType.DMA
    f32, bf16 = jnp.float32, jnp.bfloat16
    hold, shifted = pl.pallas_call(
        functools.partial(step_kernel, n_row, n_col),
        out_shape=(
            jax.ShapeDtypeStruct((PANEL, width), f32),
            jax.ShapeDtypeStruct((height, 2 * PANEL), bf16),
        ),
        in_specs=[pl.BlockSpec(memory_space=pltpu.HBM)],
        out_specs=(pl.BlockSpec(memory_space=pltpu.VMEM),) * 2,
        scratch_shapes=[
            pltpu.VMEM((height, width), f32),
            pltpu.VMEM((PANEL, width), f32),
            pltpu.VMEM((pairs, PANEL, LANES), f32),
            pltpu.VMEM((pairs + ups, PANEL, LANES), f32),
            pltpu.VMEM((most, PANEL, LANES), f32),
            pltpu.VMEM((2 * PANEL, height), bf16),
            pltpu.VMEM((height, PANEL), f32),
            pltpu.VMEM((PANEL, PANEL), f32),
            pltpu.VMEM((PANEL, PANEL), f32),
            pltpu.VMEM((PANEL, 2 * PANEL), f32),
            pltpu.VMEM((n_row, piece, PANEL), f32),
            pltpu.VMEM((n_row - 1, piece, PANEL), f32),
            pltpu.VMEM((n_row, piece, PANEL), f32),
            dma((1,)),
            dma((blocks,)),
            dma((1,)),
            dma((n_col,)),
            dma((1,)),
            dma((1,)),
            dma((1,)),
            dma((1,)),
            dma((1,)),
            dma((1,)),
            dma((1,)),
            dma((1,)),
            dma((2,)),
            dma((1,)),
            dma((most,)),
            dma((1,)),
            dma((pairs,)),
            dma((1,)),
            dma((pairs + ups,)),
            dma((1,)),
            dma((pairs,)),
            dma((1,)),
            dma((pairs + ups,)),
        ],
        compiler_params=pltpu.CompilerParams(
            collective_id=0, has_side_effects=True, vmem_limit_bytes=44 * 1024 * 1024
        ),
        name="whole_step",
    )(matrix)
    return flush(matrix, hold, shifted)


def solution(mesh):
    body = functools.partial(on_device, mesh.shape["row"], mesh.shape["col"])
    return jax.shard_map(body, mesh=mesh, in_specs=(P("row", "col"),), out_specs=P("row", "col"), check_vma=False)
```

```python
import functools

import jax
import jax.numpy as jnp
from jax import lax
from jax.experimental import pallas as pl
from jax.experimental.pallas import tpu as pltpu
from jax.sharding import PartitionSpec as P

PANEL = 128
STRIP = 8
LANES = 128
MESH = pl.DeviceIdType.MESH
EARLY = 8
LATE = 7
UP_SHARE = 5
UPDATES = 6
LEAD_PACE = 2.5
HOP = 4.1
UPDATE_LAG = 6.0


def dot_exact(a, b, contract):
    return lax.dot_general(
        a, b, (contract, ((), ())), precision=lax.Precision.HIGHEST, preferred_element_type=jnp.float32
    )


def factor_values(gram, top, between=lambda strip: None):
    strips = PANEL // STRIP
    shape = (STRIP, LANES)
    rows = lax.broadcasted_iota(jnp.int32, shape, 0)
    lanes = lax.broadcasted_iota(jnp.int32, shape, 1)
    eye = (
        lax.broadcasted_iota(jnp.int32, (PANEL, PANEL), 0) == lax.broadcasted_iota(jnp.int32, (PANEL, PANEL), 1)
    ).astype(jnp.float32)
    chol = jnp.concatenate([gram, eye], axis=1)
    work = jnp.concatenate([top, jnp.zeros_like(top)], axis=1)
    factor_rows = []
    previous = None

    def spread(x, start):
        return [jnp.broadcast_to(x[:, start + c : start + c + 1], shape) for c in range(STRIP)]

    for strip in range(strips + 1):
        at, back = strip * STRIP, (strip - 1) * STRIP
        if strip < strips:
            between(strip)
            panel = chol[:STRIP]
            columns = spread(panel, at)
            halves = [panel[:, :LANES], panel[:, LANES:]]
            scale = jnp.ones(shape, jnp.float32)
        if strip > 0:
            inner = work[back : back + STRIP] + previous
            aside = work[:, back : back + STRIP]
            inner_columns = spread(inner, back)
            inner_halves = [inner[:, :LANES], inner[:, LANES:]]
        for j in range(STRIP):
            if strip < strips:
                pivot = columns[j][j : j + 1]
                multiplier = jnp.where(rows > j, columns[j] * (1.0 / pivot), 0.0)
                scale = jnp.where(rows == j, lax.rsqrt(pivot), scale)
                columns = [x if c <= j else x - multiplier * x[j : j + 1] for c, x in enumerate(columns)]
                halves = [x - multiplier * x[j : j + 1] for x in halves]
            if strip > 0:
                column = inner_columns[j]
                inverse = 1.0 / column[j : j + 1]

                def eliminate(x):
                    pivot_row = x[j : j + 1] * inverse
                    return jnp.where(rows == j, pivot_row, x - column * pivot_row)

                inner_columns = [x if c <= j else eliminate(x) for c, x in enumerate(inner_columns)]
                inner_halves = [eliminate(x) for x in inner_halves]
        if strip < strips:
            halves = [halves[0] * scale, halves[1] * scale]
            halves[0] = jnp.where(lanes >= at + rows, halves[0], 0.0)
            panel = jnp.concatenate(halves, axis=1)
            factor_rows.append(halves[0])
            if strip < strips - 1:
                chol = chol[STRIP:] - dot_exact(panel[:, at + STRIP : PANEL], panel, ((0,), (0,)))
        if strip > 0:
            inner = jnp.concatenate(inner_halves, axis=1)
            update = dot_exact(aside, inner, ((1,), (0,)))
            pieces = []
            if back > 0:
                pieces.append(work[:back] - update[:back])
            pieces.append(inner)
            if strip < strips:
                pieces.append(work[at:] - update[at:])
            work = jnp.concatenate(pieces, axis=0)
        previous = panel
    return jnp.concatenate(factor_rows, axis=0), work[:, PANEL:]


def send(src, dst, send_sem, recv_sem, target):
    return pltpu.make_async_remote_copy(
        src_ref=src, dst_ref=dst, send_sem=send_sem, recv_sem=recv_sem, device_id=target, device_id_type=MESH
    )


def split(x):
    high = x.astype(jnp.bfloat16)
    return high, (x - high.astype(jnp.float32)).astype(jnp.bfloat16)


def product(shifted, values):
    high, low = split(values)
    both = jnp.dot(shifted[...], jnp.concatenate([high, high], axis=0), preferred_element_type=jnp.float32)
    return both + jnp.dot(shifted[:, :PANEL], low, preferred_element_type=jnp.float32)


def owned_counts(pairs):
    return pairs - pairs // UP_SHARE, pairs // UP_SHARE


def slot_of(i, owner, n_up):
    if owner == 1:
        return 2 * i + 1
    return 2 * i if i < n_up else i + n_up


def is_direct(i, owner):
    return owner == 1


def plan(role, counts, prompt):
    events = []

    def put(time, kind, owner, i):
        events.append((time, len(events), (kind, owner, i)))

    held = [0, 0]
    turns = sorted((slot_of(i, owner, counts[1]), owner, i) for owner in range(2) for i in range(counts[owner]))
    for p, owner, i in turns:
        after = held[owner]
        if p >= prompt:
            held[owner] += 1
            if role == 0:
                put(26.0 + 0.1 * i if owner == 1 else 27.0 + 0.7 * after, "late", owner, i)
        if owner == 0:
            sent = 31.4 + 1.5 * i
            if i < UPDATES:
                put(47.0 + i if role == 0 else sent + HOP * role + UPDATE_LAG, "update", 0, i)
            if role == 0:
                put(27.3 + 0.7 * i, "solve", 0, i)
            else:
                put(sent + HOP * role, "own", 0, i)
            if role in (1, 2):
                put(21.2 + 1.4 * i + 3.2 * (2 - role), "down", 0, i)
            continue
        near, away, join, solved = 25.0 + 2.8 * i, 29.0 + 2.8 * i, 33.0 + 2.8 * i, 37.0 + 2.4 * i
        if p >= prompt:
            near, away, join, solved = 34.0 + 3.5 * after, 37.5 + 3.5 * after, 41.0 + 3.5 * after, 46.0 + 3.0 * after
        if role == 3:
            put(solved, "solve", 1, i)
            put(solved + 4.5, "pass", 1, i)
        else:
            put(solved + 1.5 + HOP * (3 - role), "own", 1, i)
            put(solved + 2.0 + HOP * (4 - role), "other", 1, i)
        if role == 1:
            put(near, "up", 1, i)
        if role == 2:
            put(away, "up", 1, i)
            put(join, "join", 1, i)
    return [event for _, _, event in sorted(events)]


def step_kernel(
    n_row, n_col, matrix_ref, block, hold, shifted,
    partial, pair_in, chain_in, top_in, stacked, panel, top, factor_ref, inverse_ref,
    parts, arrived, whole,
    fetch_sem, block_sem, own_sem,
    panel_send, panel_recv, part_send, part_recv, whole_send, whole_recv, top_send, top_recv, share_send, share_recv,
    scatter_send, scatter_recv, pair_send, pair_recv, chain_send, chain_recv,
    give_send, give_recv, pass_send, pass_recv,
):
    row, col = lax.axis_index("row"), lax.axis_index("col")
    width = block.shape[1]
    blocks = width // (4 * LANES)
    pairs = 2 * blocks
    counts = owned_counts(pairs)
    prompt = pairs - LATE
    piece = PANEL // n_row
    outer_n = n_row // 2
    last = outer_n - 1
    outer, inner = row // 2, lax.rem(row, 2)
    other = 1 - inner
    partner = {"row": outer * 2 + other}
    first, final = outer == 0, outer == last
    is_end = first | final
    mine = jnp.where(first, 0, 1)
    near = jnp.where(2 * outer < outer_n, 0, 1)
    end_rows = [0, 1, n_row - 2, n_row - 1]

    barrier = pltpu.get_barrier_semaphore()
    for d in range(1, n_row):
        pl.semaphore_signal(barrier, inc=1, device_id={"row": lax.rem(row + d, n_row)}, device_id_type=MESH)
    for d in range(1, n_col):
        pl.semaphore_signal(barrier, inc=1, device_id={"col": lax.rem(col + d, n_col)}, device_id_type=MESH)

    def lanes(start, size):
        return pl.ds(pl.multiple_of(start, LANES), size)

    def unit(p, side):
        return lanes(p * (2 * LANES) + side * LANES, LANES)

    def load(j):
        place = lanes(j * (4 * LANES), 4 * LANES)
        return pltpu.make_async_copy(matrix_ref.at[:, place], block.at[:, place], block_sem.at[j])

    def static_slot(i, owner):
        return slot_of(i, owner, counts[1])

    def owner_of(p):
        return jnp.where((p < 2 * counts[1]) & (lax.rem(p, 2) == 1), 1, 0)

    def turn_of(p):
        if isinstance(p, int):
            return p // 2 if p < 2 * counts[1] else p - counts[1]
        return jnp.where(p < 2 * counts[1], lax.div(p, 2), p - counts[1])

    def scatter(p, side, up):
        return send(
            matrix_ref.at[pl.ds(0, PANEL), unit(p, side)], top_in.at[turn_of(p)],
            scatter_send.at[0], scatter_recv.at[turn_of(p)], {"row": end_rows[2 * up + side]},
        )

    def keep(i):
        place = unit(static_slot(i, 0), 0)
        return pltpu.make_async_copy(matrix_ref.at[pl.ds(0, PANEL), place], top_in.at[i], own_sem.at[0])

    def start_scatter(p):
        @pl.when((row == 0) & (owner_of(p) == 0) & (p < prompt))
        def _():
            scatter(p, 1, 0).start()

    def start_up(i):
        @pl.when((row == 0) & (static_slot(i, 1) < prompt))
        def _():
            for side in range(2):
                scatter(static_slot(i, 1), side, 1).start()

    def pair(p):
        return send(partial.at[:, unit(p, other)], pair_in.at[p], pair_send.at[0], pair_recv.at[p], partner)

    def chain(p, towards, own):
        slot = way(p, own)
        return send(
            partial.at[:, unit(p, inner if own else other)], chain_in.at[slot],
            chain_send.at[0], chain_recv.at[slot], {"row": row + 2 * (2 * towards - 1)},
        )

    def way(p, own):
        return p if own else pairs + turn_of(p)

    joins = outer == last - 1

    def give(p):
        place = unit(p, inner)
        return send(hold.at[:, place], hold.at[:, place], give_send.at[0], give_recv.at[p], partner)

    def given(p):
        place = unit(p, other)
        return send(hold.at[:, place], hold.at[:, place], give_send.at[0], give_recv.at[p], partner)

    def onward(p, owner, own):
        place = unit(p, inner if own else other)
        slot = way(p, own)
        return send(
            hold.at[:, place], hold.at[:, place], pass_send.at[0], pass_recv.at[slot],
            {"row": row + 2 * (1 - 2 * owner)},
        )

    def multiply(j):
        place = lanes(j * (4 * LANES), 4 * LANES)
        high, low = split(block[:, place])
        both = jnp.dot(stacked[...], high, preferred_element_type=jnp.float32)
        rest = jnp.dot(stacked[:PANEL], low, preferred_element_type=jnp.float32)
        partial[:, place] = both[:PANEL] + both[PANEL:] + rest

    def exchange(p):
        owner = owner_of(p)

        prompt_here = jnp.logical_not((row == 0) & (p >= prompt))

        @pl.when((owner == 0) & prompt_here)
        def _():
            pair(p).start()

        @pl.when((owner == 1) & first & prompt_here)
        def _():
            chain(p, owner, True).start()
            chain(p, owner, False).start()

    def exchange_last():
        @pl.when(final)
        def _():
            for i in range(counts[1]):
                pair(static_slot(i, 1)).start()

    def prepare():
        high, low = split(panel[...])
        shifted[:, :PANEL] = high
        shifted[:, PANEL:] = low
        high, low = split(jnp.transpose(panel[...]))
        stacked[:PANEL] = high
        stacked[PANEL:] = low

    def multiply_range(start, stop, ahead):
        @pl.loop(start, stop)
        def _(j):
            load(j).wait()
            multiply(j)
            for p in (2 * j, 2 * j + 1):
                exchange(p)

                @pl.when(p + ahead < pairs)
                def _():
                    start_scatter(p + ahead)

    @pl.when(col == 0)
    def _():
        fetch = pltpu.make_async_copy(matrix_ref.at[:, pl.ds(0, PANEL)], panel, fetch_sem.at[0])
        fetch.start()
        fetch.wait()
        for j in range(blocks):
            load(j).start()
        local = dot_exact(panel[...], panel[...], ((0,), (0,)))
        for q in range(n_row):
            parts[q] = local[q * piece : (q + 1) * piece]

    @pl.when(col != 0)
    def _():
        for j in range(blocks):
            load(j).start()

    @pl.when(row == 0)
    def _():
        for i in range(counts[0]):
            if static_slot(i, 0) < prompt:
                keep(i).start()

    pl.semaphore_wait(barrier, n_row - 1 + n_col - 1)

    def panel_copy(to, slot):
        return send(panel, panel, panel_send.at[slot], panel_recv.at[0], {"col": to})

    heads = [1] + [c for c in range(2, n_col, 2)]

    @pl.when(col == 0)
    def _():
        def part(d):
            q = lax.rem(row + d, n_row)
            return send(parts.at[q], arrived.at[d - 1], part_send.at[0], part_recv.at[0], {"row": q})

        def whole_copy(e):
            return send(whole.at[row], whole.at[row], whole_send.at[0], whole_recv.at[0], {"row": end_rows[e]})

        def top_copy(e):
            return send(panel.at[pl.ds(0, PANEL)], top, top_send.at[0], top_recv.at[0], {"row": end_rows[e]})

        def share(c, slot):
            ref = (top, whole)[slot]
            return send(ref, ref, share_send.at[0], share_recv.at[slot], {"col": c})

        for d in range(1, n_row):
            part(d).start()
        for slot, c in enumerate(heads[1:]):
            panel_copy(c, slot + 1).start()

        @pl.when(row == 0)
        def _():
            for e in range(1, 4):
                top_copy(e).start()
            top[...] = panel[:PANEL]

        prepare()

        @pl.loop(0, blocks // 2)
        def _(j):
            load(j).wait()
            multiply(j)

        send(arrived, arrived, part_send.at[0], part_recv.at[0], {"row": 0}).wait_recv()
        total = parts[row]
        for d in range(1, n_row):
            total = total + arrived[d - 1]
        whole[row] = total
        for e in range(4):
            @pl.when(row != end_rows[e])
            def _():
                whole_copy(e).start()

        panel_copy(heads[0], 0).start()
        for i in range(counts[1]):
            start_up(i)

        @pl.loop(0, 2 * (blocks // 2))
        def _(p):
            exchange(p)

            start_scatter(p)

        @pl.when(is_end)
        def _():
            @pl.when(row != 0)
            def _():
                send(top, top, top_send.at[0], top_recv.at[0], {"row": 0}).wait_recv()

            for c in range(1, n_col):
                share(c, 0).start()

        multiply_range(blocks // 2, blocks, 0)
        exchange_last()

        @pl.when(is_end)
        def _():
            most = whole.at[pl.ds(0, n_row - 1)]
            send(most, most, whole_send.at[0], whole_recv.at[0], {"row": 0}).wait_recv()
            for c in range(1, n_col):
                share(c, 1).start()

    @pl.when(col != 0)
    def _():
        @pl.when(col != 1)
        def _():
            for p in range(EARLY):
                start_scatter(p)
            for i in range(counts[1]):
                start_up(i)

        root = {"col": 0}
        send(panel, panel, panel_send.at[0], panel_recv.at[0], root).wait_recv()
        relay = (lax.rem(col, 2) == 0) & (col + 1 < n_col)

        @pl.when(relay)
        def _():
            panel_copy(col + 1, 0).start()

        @pl.when(col == 1)
        def _():
            for i in range(counts[1]):
                start_up(i)

        prepare()
        ahead = jnp.where(col == 1, 0, EARLY)
        multiply_range(0, blocks, ahead)
        exchange_last()

        @pl.when(is_end)
        def _():
            send(top, top, share_send.at[0], share_recv.at[0], root).wait_recv()
            send(whole, whole, share_send.at[0], share_recv.at[1], root).wait_recv()

        @pl.when(relay)
        def _():
            panel_copy(col + 1, 0).wait_send()

    def add(p, side, *terms):
        place = unit(p, side)
        total = partial[:, place]
        for term in terms:
            total = total + term[...]
        partial[:, place] = total

    def lead(i):
        p = static_slot(i, 0)
        pair(p).wait_recv()
        add(p, inner, pair_in.at[p])
        chain(p, 0, True).start()

    def relay_down(i):
        p = static_slot(i, 0)
        pair(p).wait_recv()
        chain(p, 0, True).wait_recv()
        add(p, inner, pair_in.at[p], chain_in.at[p])
        chain(p, 0, True).start()

    def relay_up(i):
        p = static_slot(i, 1)
        for own in (False, True):
            chain(p, 1, own).wait_recv()
            add(p, inner if own else other, chain_in.at[way(p, own)])

            @pl.when(jnp.logical_not(joins))
            def _():
                chain(p, 1, own).start()

            if not own:
                @pl.when(joins)
                def _():
                    pair(p).start()

    def join_up(i):
        @pl.when(joins)
        def _():
            p = static_slot(i, 1)
            pair(p).wait_recv()
            add(p, inner, pair_in.at[p])
            chain(p, 1, True).start()

    @pl.when(is_end)
    def _():
        gram = jnp.concatenate([whole[q] for q in range(n_row)], axis=0)

        strips = [2 + int(LEAD_PACE * i) for i in range(counts[0])]

        def between(strip):
            if strip in strips:
                @pl.when(final)
                def _():
                    lead(strips.index(strip))

        factor, inverse = factor_values(gram, top[...], between)
        factor_ref[...] = factor
        inverse_ref[:, :PANEL] = inverse
        inverse_ref[:, PANEL:] = dot_exact(inverse, factor, ((1,), (1,)))

        @pl.when(final)
        def _():
            for i in range(counts[0]):
                if strips[i] >= PANEL // STRIP:
                    lead(i)

        @pl.when(row == 0)
        def _():
            high, low = split(panel[:PANEL] + factor)
            shifted[:PANEL, :PANEL] = high
            shifted[:PANEL, PANEL:] = low

    def update(i):
        p = static_slot(i, 0)
        given(p).wait_recv()
        place = pl.ds(p * (2 * LANES), 2 * LANES)
        block[:, place] = block[:, place] - product(shifted, hold[:, place])

    def late(i, owner):
        p = static_slot(i, owner)

        @pl.when(row == 0)
        def _():
            place = unit(p, 1) if owner == 0 else lanes(p * (2 * LANES), 2 * LANES)
            extra = dot_exact(factor_ref[...], block[:PANEL, place], ((0,), (0,)))
            partial[:, place] = partial[:, place] + extra
            if owner == 0:
                pair(p).start()
            else:
                chain(p, 1, True).start()
                chain(p, 1, False).start()

    def solve(i, owner):
        p = static_slot(i, owner)
        pair(p).wait_recv()
        chain(p, owner, True).wait_recv()
        place = unit(p, inner)
        held = p >= prompt

        def at_row_zero():
            if held:
                top_in[i] = block[:PANEL, place]

        def elsewhere():
            if held:
                top_in[i] = jnp.zeros((PANEL, LANES), jnp.float32)
            else:
                send(top_in.at[i], top_in.at[i], scatter_send.at[0], scatter_recv.at[i], {"row": 0}).wait_recv()

        if owner == 0:
            pl.when(row == 0)(at_row_zero)
            pl.when(row != 0)(elsewhere)
        else:
            elsewhere()
        total = partial[:, place] + pair_in[p] + chain_in[p]
        hold[:, place] = dot_exact(inverse_ref[...], jnp.concatenate([total, top_in[i]], axis=0), ((1,), (0,)))
        onward(p, owner, True).start()
        give(p).start()

    def pass_other(i, owner):
        p = static_slot(i, owner)
        given(p).wait_recv()
        onward(p, owner, False).start()

    def accept(i, owner, own, stops):
        p = static_slot(i, owner)
        onward(p, owner, own).wait_recv()
        if not stops:
            onward(p, owner, own).start()
        if own and not is_direct(i, owner):
            give(p).start()

    turns = sorted((static_slot(i, owner), owner, i) for owner in range(2) for i in range(counts[owner]))

    def drain(sem, units):
        ref = partial.at[:, pl.ds(0, units * LANES)]
        send(ref, ref, sem.at[0], pair_recv.at[0], partner).wait_send()

    downs, ups = counts
    prompt_downs = sum(1 for p, owner, _ in turns if owner == 0 and p < prompt)
    prompt_ups = sum(1 for p, owner, _ in turns if owner == 1 and p < prompt)

    def settle(role):
        for p, owner, i in turns:
            if not is_direct(i, owner) and i >= UPDATES:
                given(p).wait_recv()
        drain(give_send, downs + (ups if role == 3 else 0))
        drain(pass_send, (downs, downs + 2 * ups, downs + 2 * ups, 2 * ups)[role])
        if role == 2:
            @pl.when(joins)
            def _():
                drain(pair_send, downs + ups)
                drain(chain_send, downs + ups)

            @pl.when(jnp.logical_not(joins))
            def _():
                drain(pair_send, downs)
                drain(chain_send, downs + 2 * ups)
        else:
            drain(pair_send, downs + (ups if role == 3 else 0))
            drain(chain_send, (2 * ups, downs + 2 * ups, 0, downs)[role])
        if role == 0:
            @pl.when(row == 0)
            def _():
                drain(scatter_send, prompt_downs + 2 * prompt_ups)

        @pl.when(col == 0)
        def _():
            for slot, c in enumerate(heads):
                panel_copy(c, slot).wait_send()
            send(arrived, arrived, part_send.at[0], part_recv.at[0], {"row": 0}).wait_send()
            sent = whole.at[pl.ds(0, 3 if role in (0, 3) else 4)]
            send(sent, sent, whole_send.at[0], whole_recv.at[0], {"row": 0}).wait_send()
            if role in (0, 3):
                drain(share_send, 2 * (n_col - 1))
            if role == 0:
                @pl.when(row == 0)
                def _():
                    drain(top_send, 3)

    def follow(role):
        if role == 0:
            @pl.when(row == 0)
            def _():
                kept = top_in.at[pl.ds(0, prompt_downs)]
                pltpu.make_async_copy(kept, kept, own_sem.at[0]).wait()

        for event in plan(role, counts, prompt):
            kind, owner, i = event
            if kind == "solve":
                solve(i, owner)
            elif kind == "late":
                late(i, owner)
            elif kind == "update":
                update(i)
            elif kind == "pass":
                pass_other(i, owner)
            elif kind == "down":
                relay_down(i)
            elif kind == "up":
                relay_up(i)
            elif kind == "join":
                join_up(i)
            else:
                accept(i, owner, kind == "own", role == (3, 0)[owner])
        settle(role)

    pl.when(first)(lambda: follow(0))
    pl.when(jnp.logical_not(is_end) & (near == 0))(lambda: follow(1))
    pl.when(jnp.logical_not(is_end) & (near == 1))(lambda: follow(2))
    pl.when(final)(lambda: follow(3))


def flush_kernel(n_up, block, hold, shifted, out, ring, sem, done_sem):
    slots = ring.shape[0]
    rest = out.shape[1] // (2 * LANES) - UPDATES

    def lanes(p):
        return pl.ds(p * (2 * LANES) if isinstance(p, int) else pl.multiple_of(p * (2 * LANES), LANES), 2 * LANES)

    def place(r):
        return lanes(jnp.where(r < n_up, 2 * r + 1, r + UPDATES))

    def store(r):
        slot = lax.rem(r, slots)
        return pltpu.make_async_copy(ring.at[slot], out.at[:, place(r)], sem.at[slot])

    def done(i):
        where = lanes(slot_of(i, 0, n_up))
        return pltpu.make_async_copy(block.at[:, where], out.at[:, where], done_sem.at[i])

    for i in range(UPDATES):
        done(i).start()

    @pl.loop(0, rest)
    def _(r):
        @pl.when(r >= slots)
        def _():
            store(r - slots).wait()

        ring[lax.rem(r, slots)] = block[:, place(r)] - product(shifted, hold[:, place(r)])
        store(r).start()

    for i in range(UPDATES):
        done(i).wait()

    @pl.loop(rest - slots, rest)
    def _(r):
        store(r).wait()


def flush(block, hold, shifted, n_up):
    height, width = block.shape
    vmem = pl.BlockSpec(memory_space=pltpu.VMEM)
    return pl.pallas_call(
        functools.partial(flush_kernel, n_up),
        out_shape=jax.ShapeDtypeStruct(block.shape, block.dtype),
        in_specs=[vmem] * 3,
        out_specs=pl.BlockSpec(memory_space=pl.ANY),
        scratch_shapes=[
            pltpu.VMEM((4, height, 2 * LANES), jnp.float32),
            pltpu.SemaphoreType.DMA((4,)),
            pltpu.SemaphoreType.DMA((UPDATES,)),
        ],
        compiler_params=pltpu.CompilerParams(vmem_limit_bytes=16 * 1024 * 1024),
        name="flush",
    )(block, hold, shifted)


def on_device(n_row, n_col, matrix):
    height, width = matrix.shape
    piece = PANEL // n_row
    blocks = width // (4 * LANES)
    pairs = 2 * blocks
    most, ups = owned_counts(pairs)
    dma = pltpu.SemaphoreType.DMA
    f32, bf16 = jnp.float32, jnp.bfloat16
    block, hold, shifted = pl.pallas_call(
        functools.partial(step_kernel, n_row, n_col),
        out_shape=(
            jax.ShapeDtypeStruct((height, width), f32),
            jax.ShapeDtypeStruct((PANEL, width), f32),
            jax.ShapeDtypeStruct((height, 2 * PANEL), bf16),
        ),
        in_specs=[pl.BlockSpec(memory_space=pltpu.HBM)],
        out_specs=(pl.BlockSpec(memory_space=pltpu.VMEM),) * 3,
        scratch_shapes=[
            pltpu.VMEM((PANEL, width), f32),
            pltpu.VMEM((pairs, PANEL, LANES), f32),
            pltpu.VMEM((pairs + ups, PANEL, LANES), f32),
            pltpu.VMEM((most, PANEL, LANES), f32),
            pltpu.VMEM((2 * PANEL, height), bf16),
            pltpu.VMEM((height, PANEL), f32),
            pltpu.VMEM((PANEL, PANEL), f32),
            pltpu.VMEM((PANEL, PANEL), f32),
            pltpu.VMEM((PANEL, 2 * PANEL), f32),
            pltpu.VMEM((n_row, piece, PANEL), f32),
            pltpu.VMEM((n_row - 1, piece, PANEL), f32),
            pltpu.VMEM((n_row, piece, PANEL), f32),
            dma((1,)),
            dma((blocks,)),
            dma((1,)),
            dma((n_col,)),
            dma((1,)),
            dma((1,)),
            dma((1,)),
            dma((1,)),
            dma((1,)),
            dma((1,)),
            dma((1,)),
            dma((1,)),
            dma((2,)),
            dma((1,)),
            dma((most,)),
            dma((1,)),
            dma((pairs,)),
            dma((1,)),
            dma((pairs + ups,)),
            dma((1,)),
            dma((pairs,)),
            dma((1,)),
            dma((pairs + ups,)),
        ],
        compiler_params=pltpu.CompilerParams(
            collective_id=0, has_side_effects=True, vmem_limit_bytes=36 * 1024 * 1024
        ),
        name="whole_step",
    )(matrix)
    return flush(block, hold, shifted, owned_counts(pairs)[1])


def solution(mesh):
    body = functools.partial(on_device, mesh.shape["row"], mesh.shape["col"])
    return jax.shard_map(body, mesh=mesh, in_specs=(P("row", "col"),), out_specs=P("row", "col"), check_vma=False)
```

```python
import functools

import jax
import jax.numpy as jnp
from jax import lax
from jax.experimental import pallas as pl
from jax.experimental.pallas import tpu as pltpu
from jax.sharding import PartitionSpec as P

PANEL = 128
STRIP = 8
LANES = 128
MESH = pl.DeviceIdType.MESH
EARLY = 8
LATE = 7
UP_SHARE = 5
UPDATES = 6
LEAD_PACE = 1.6
HOP = 4.1
UPDATE_LAG = 6.0


def dot_exact(a, b, contract):
    return lax.dot_general(
        a, b, (contract, ((), ())), precision=lax.Precision.HIGHEST, preferred_element_type=jnp.float32
    )


def factor_values(gram, top, between=lambda strip: None):
    strips = PANEL // STRIP
    shape = (STRIP, LANES)
    rows = lax.broadcasted_iota(jnp.int32, shape, 0)
    lanes = lax.broadcasted_iota(jnp.int32, shape, 1)
    eye = (
        lax.broadcasted_iota(jnp.int32, (PANEL, PANEL), 0) == lax.broadcasted_iota(jnp.int32, (PANEL, PANEL), 1)
    ).astype(jnp.float32)
    chol = jnp.concatenate([gram, eye], axis=1)
    work = jnp.concatenate([top, jnp.zeros_like(top)], axis=1)
    factor_rows = []
    previous = None

    def spread(x, start):
        return [jnp.broadcast_to(x[:, start + c : start + c + 1], shape) for c in range(STRIP)]

    for strip in range(strips + 1):
        at, back = strip * STRIP, (strip - 1) * STRIP
        if strip < strips:
            between(strip)
            panel = chol[:STRIP]
            columns = spread(panel, at)
            halves = [panel[:, :LANES], panel[:, LANES:]]
            scale = jnp.ones(shape, jnp.float32)
        if strip > 0:
            inner = work[back : back + STRIP] + previous
            aside = work[:, back : back + STRIP]
            inner_columns = spread(inner, back)
            inner_halves = [inner[:, :LANES], inner[:, LANES:]]
        for j in range(STRIP):
            if strip < strips:
                pivot = columns[j][j : j + 1]
                multiplier = jnp.where(rows > j, columns[j] * (1.0 / pivot), 0.0)
                scale = jnp.where(rows == j, lax.rsqrt(pivot), scale)
                columns = [x if c <= j else x - multiplier * x[j : j + 1] for c, x in enumerate(columns)]
                halves = [x - multiplier * x[j : j + 1] for x in halves]
            if strip > 0:
                column = inner_columns[j]
                inverse = 1.0 / column[j : j + 1]

                def eliminate(x):
                    pivot_row = x[j : j + 1] * inverse
                    return jnp.where(rows == j, pivot_row, x - column * pivot_row)

                inner_columns = [x if c <= j else eliminate(x) for c, x in enumerate(inner_columns)]
                inner_halves = [eliminate(x) for x in inner_halves]
        if strip < strips:
            halves = [halves[0] * scale, halves[1] * scale]
            halves[0] = jnp.where(lanes >= at + rows, halves[0], 0.0)
            panel = jnp.concatenate(halves, axis=1)
            factor_rows.append(halves[0])
            if strip < strips - 1:
                chol = chol[STRIP:] - dot_exact(panel[:, at + STRIP : PANEL], panel, ((0,), (0,)))
        if strip > 0:
            inner = jnp.concatenate(inner_halves, axis=1)
            update = dot_exact(aside, inner, ((1,), (0,)))
            pieces = []
            if back > 0:
                pieces.append(work[:back] - update[:back])
            pieces.append(inner)
            if strip < strips:
                pieces.append(work[at:] - update[at:])
            work = jnp.concatenate(pieces, axis=0)
        previous = panel
    return jnp.concatenate(factor_rows, axis=0), work[:, PANEL:]


def send(src, dst, send_sem, recv_sem, target):
    return pltpu.make_async_remote_copy(
        src_ref=src, dst_ref=dst, send_sem=send_sem, recv_sem=recv_sem, device_id=target, device_id_type=MESH
    )


def split(x):
    high = x.astype(jnp.bfloat16)
    return high, (x - high.astype(jnp.float32)).astype(jnp.bfloat16)


def product(shifted, values):
    high, low = split(values)
    both = jnp.dot(shifted[...], jnp.concatenate([high, high], axis=0), preferred_element_type=jnp.float32)
    return both + jnp.dot(shifted[:, :PANEL], low, preferred_element_type=jnp.float32)


def owned_counts(pairs):
    return pairs - pairs // UP_SHARE, pairs // UP_SHARE


def slot_of(i, owner, n_up):
    if owner == 1:
        return 2 * i + 1
    return 2 * i if i < n_up else i + n_up


def is_direct(i, owner):
    return owner == 1


def plan(role, counts, prompt):
    events = []

    def put(time, kind, owner, i):
        events.append((time, len(events), (kind, owner, i)))

    held = [0, 0]
    turns = sorted((slot_of(i, owner, counts[1]), owner, i) for owner in range(2) for i in range(counts[owner]))
    for p, owner, i in turns:
        after = held[owner]
        if p >= prompt:
            held[owner] += 1
            if role == 0:
                put(26.0 + 0.1 * i if owner == 1 else 27.0 + 0.7 * after, "late", owner, i)
        if owner == 0:
            sent = 31.4 + 1.5 * i
            if i < UPDATES:
                put(47.0 + i if role == 0 else sent + HOP * role + UPDATE_LAG, "update", 0, i)
            if role == 0:
                put(27.3 + 0.7 * i, "solve", 0, i)
            else:
                put(sent + HOP * role, "own", 0, i)
            if role in (1, 2):
                put(21.2 + 1.4 * i + 3.2 * (2 - role), "down", 0, i)
            continue
        near, away, join, solved = 25.0 + 2.8 * i, 29.0 + 2.8 * i, 33.0 + 2.8 * i, 37.0 + 2.4 * i
        if p >= prompt:
            near, away, join, solved = 34.0 + 3.5 * after, 37.5 + 3.5 * after, 41.0 + 3.5 * after, 46.0 + 3.0 * after
        if role == 3:
            put(solved, "solve", 1, i)
            put(solved + 8.0, "pass", 1, i)
        else:
            put(solved + 1.5 + HOP * (3 - role), "own", 1, i)
            put(solved + 5.0 + HOP * (4 - role), "other", 1, i)
        if role == 1:
            put(near, "up", 1, i)
        if role == 2:
            put(away, "up", 1, i)
            put(join, "join", 1, i)
    return [event for _, _, event in sorted(events)]


def step_kernel(
    n_row, n_col, matrix_ref, block, hold, shifted,
    partial, pair_in, chain_in, top_in, stacked, panel, top, factor_ref, inverse_ref,
    parts, arrived, whole,
    fetch_sem, block_sem, own_sem,
    panel_send, panel_recv, part_send, part_recv, whole_send, whole_recv, top_send, top_recv, share_send, share_recv,
    scatter_send, scatter_recv, pair_send, pair_recv, chain_send, chain_recv,
    give_send, give_recv, pass_send, pass_recv,
):
    row, col = lax.axis_index("row"), lax.axis_index("col")
    width = block.shape[1]
    blocks = width // (4 * LANES)
    pairs = 2 * blocks
    counts = owned_counts(pairs)
    prompt = pairs - LATE
    piece = PANEL // n_row
    outer_n = n_row // 2
    last = outer_n - 1
    outer, inner = row // 2, lax.rem(row, 2)
    other = 1 - inner
    partner = {"row": outer * 2 + other}
    first, final = outer == 0, outer == last
    is_end = first | final
    mine = jnp.where(first, 0, 1)
    near = jnp.where(2 * outer < outer_n, 0, 1)
    end_rows = [0, 1, n_row - 2, n_row - 1]

    barrier = pltpu.get_barrier_semaphore()
    for d in range(1, n_row):
        pl.semaphore_signal(barrier, inc=1, device_id={"row": lax.rem(row + d, n_row)}, device_id_type=MESH)
    for d in range(1, n_col):
        pl.semaphore_signal(barrier, inc=1, device_id={"col": lax.rem(col + d, n_col)}, device_id_type=MESH)

    def lanes(start, size):
        return pl.ds(pl.multiple_of(start, LANES), size)

    def unit(p, side):
        return lanes(p * (2 * LANES) + side * LANES, LANES)

    def load(j):
        place = lanes(j * (4 * LANES), 4 * LANES)
        return pltpu.make_async_copy(matrix_ref.at[:, place], block.at[:, place], block_sem.at[j])

    def static_slot(i, owner):
        return slot_of(i, owner, counts[1])

    def owner_of(p):
        return jnp.where((p < 2 * counts[1]) & (lax.rem(p, 2) == 1), 1, 0)

    def turn_of(p):
        if isinstance(p, int):
            return p // 2 if p < 2 * counts[1] else p - counts[1]
        return jnp.where(p < 2 * counts[1], lax.div(p, 2), p - counts[1])

    def scatter(p, side, up):
        return send(
            matrix_ref.at[pl.ds(0, PANEL), unit(p, side)], top_in.at[turn_of(p)],
            scatter_send.at[0], scatter_recv.at[turn_of(p)], {"row": end_rows[2 * up + side]},
        )

    def keep(i):
        place = unit(static_slot(i, 0), 0)
        return pltpu.make_async_copy(matrix_ref.at[pl.ds(0, PANEL), place], top_in.at[i], own_sem.at[0])

    def start_scatter(p):
        @pl.when((row == 0) & (owner_of(p) == 0) & (p < prompt))
        def _():
            scatter(p, 1, 0).start()

    def start_up(i):
        @pl.when((row == 0) & (static_slot(i, 1) < prompt))
        def _():
            for side in range(2):
                scatter(static_slot(i, 1), side, 1).start()

    def pair(p):
        return send(partial.at[:, unit(p, other)], pair_in.at[p], pair_send.at[0], pair_recv.at[p], partner)

    def chain(p, towards, own):
        slot = way(p, own)
        return send(
            partial.at[:, unit(p, inner if own else other)], chain_in.at[slot],
            chain_send.at[0], chain_recv.at[slot], {"row": row + 2 * (2 * towards - 1)},
        )

    def way(p, own):
        return p if own else pairs + turn_of(p)

    joins = outer == last - 1

    def give(p):
        place = unit(p, inner)
        return send(hold.at[:, place], hold.at[:, place], give_send.at[0], give_recv.at[p], partner)

    def given(p):
        place = unit(p, other)
        return send(hold.at[:, place], hold.at[:, place], give_send.at[0], give_recv.at[p], partner)

    def onward(p, owner, own):
        place = unit(p, inner if own else other)
        slot = way(p, own)
        return send(
            hold.at[:, place], hold.at[:, place], pass_send.at[0], pass_recv.at[slot],
            {"row": row + 2 * (1 - 2 * owner)},
        )

    def multiply(j):
        place = lanes(j * (4 * LANES), 4 * LANES)
        high, low = split(block[:, place])
        both = jnp.dot(stacked[...], high, preferred_element_type=jnp.float32)
        rest = jnp.dot(stacked[:PANEL], low, preferred_element_type=jnp.float32)
        partial[:, place] = both[:PANEL] + both[PANEL:] + rest

    def exchange(p):
        owner = owner_of(p)

        prompt_here = jnp.logical_not((row == 0) & (p >= prompt))

        @pl.when((owner == 0) & prompt_here)
        def _():
            pair(p).start()

        @pl.when((owner == 1) & first & prompt_here)
        def _():
            chain(p, owner, True).start()
            chain(p, owner, False).start()

    def exchange_last():
        @pl.when(final)
        def _():
            for i in range(counts[1]):
                pair(static_slot(i, 1)).start()

    def prepare():
        high, low = split(panel[...])
        shifted[:, :PANEL] = high
        shifted[:, PANEL:] = low
        high, low = split(jnp.transpose(panel[...]))
        stacked[:PANEL] = high
        stacked[PANEL:] = low

    def multiply_range(start, stop, ahead):
        @pl.loop(start, stop)
        def _(j):
            load(j).wait()
            multiply(j)
            for p in (2 * j, 2 * j + 1):
                exchange(p)

                @pl.when(p + ahead < pairs)
                def _():
                    start_scatter(p + ahead)

    @pl.when(col == 0)
    def _():
        fetch = pltpu.make_async_copy(matrix_ref.at[:, pl.ds(0, PANEL)], panel, fetch_sem.at[0])
        fetch.start()
        fetch.wait()
        for j in range(blocks):
            load(j).start()
        local = dot_exact(panel[...], panel[...], ((0,), (0,)))
        for q in range(n_row):
            parts[q] = local[q * piece : (q + 1) * piece]

    @pl.when(col != 0)
    def _():
        for j in range(blocks):
            load(j).start()

    @pl.when(row == 0)
    def _():
        for i in range(counts[0]):
            if static_slot(i, 0) < prompt:
                keep(i).start()

    pl.semaphore_wait(barrier, n_row - 1 + n_col - 1)

    def panel_copy(to, slot):
        return send(panel, panel, panel_send.at[slot], panel_recv.at[0], {"col": to})

    heads = [1] + [c for c in range(2, n_col, 2)]

    @pl.when(col == 0)
    def _():
        def part(d):
            q = lax.rem(row + d, n_row)
            return send(parts.at[q], arrived.at[d - 1], part_send.at[0], part_recv.at[0], {"row": q})

        def whole_copy(e):
            return send(whole.at[row], whole.at[row], whole_send.at[0], whole_recv.at[0], {"row": end_rows[e]})

        def top_copy(e):
            return send(panel.at[pl.ds(0, PANEL)], top, top_send.at[0], top_recv.at[0], {"row": end_rows[e]})

        def share(c, slot):
            ref = (top, whole)[slot]
            return send(ref, ref, share_send.at[0], share_recv.at[slot], {"col": c})

        for d in range(1, n_row):
            part(d).start()
        for slot, c in enumerate(heads[1:]):
            panel_copy(c, slot + 1).start()

        @pl.when(row == 0)
        def _():
            for e in range(1, 4):
                top_copy(e).start()
            top[...] = panel[:PANEL]

        prepare()

        @pl.loop(0, blocks // 2)
        def _(j):
            load(j).wait()
            multiply(j)

        send(arrived, arrived, part_send.at[0], part_recv.at[0], {"row": 0}).wait_recv()
        total = parts[row]
        for d in range(1, n_row):
            total = total + arrived[d - 1]
        whole[row] = total
        for e in range(4):
            @pl.when(row != end_rows[e])
            def _():
                whole_copy(e).start()

        panel_copy(heads[0], 0).start()
        for i in range(counts[1]):
            start_up(i)

        @pl.loop(0, 2 * (blocks // 2))
        def _(p):
            exchange(p)

            start_scatter(p)

        @pl.when(is_end)
        def _():
            @pl.when(row != 0)
            def _():
                send(top, top, top_send.at[0], top_recv.at[0], {"row": 0}).wait_recv()

            for c in range(1, n_col):
                share(c, 0).start()

        multiply_range(blocks // 2, blocks, 0)
        exchange_last()

        @pl.when(is_end)
        def _():
            most = whole.at[pl.ds(0, n_row - 1)]
            send(most, most, whole_send.at[0], whole_recv.at[0], {"row": 0}).wait_recv()
            for c in range(1, n_col):
                share(c, 1).start()

    @pl.when(col != 0)
    def _():
        @pl.when(col != 1)
        def _():
            for p in range(EARLY):
                start_scatter(p)
            for i in range(counts[1]):
                start_up(i)

        root = {"col": 0}
        send(panel, panel, panel_send.at[0], panel_recv.at[0], root).wait_recv()
        relay = (lax.rem(col, 2) == 0) & (col + 1 < n_col)

        @pl.when(relay)
        def _():
            panel_copy(col + 1, 0).start()

        @pl.when(col == 1)
        def _():
            for i in range(counts[1]):
                start_up(i)

        prepare()
        ahead = jnp.where(col == 1, 0, EARLY)
        multiply_range(0, blocks, ahead)
        exchange_last()

        @pl.when(is_end)
        def _():
            send(top, top, share_send.at[0], share_recv.at[0], root).wait_recv()
            send(whole, whole, share_send.at[0], share_recv.at[1], root).wait_recv()

        @pl.when(relay)
        def _():
            panel_copy(col + 1, 0).wait_send()

    def add(p, side, *terms):
        place = unit(p, side)
        total = partial[:, place]
        for term in terms:
            total = total + term[...]
        partial[:, place] = total

    def lead(i):
        p = static_slot(i, 0)
        pair(p).wait_recv()
        add(p, inner, pair_in.at[p])
        chain(p, 0, True).start()

    def relay_down(i):
        p = static_slot(i, 0)
        pair(p).wait_recv()
        chain(p, 0, True).wait_recv()
        add(p, inner, pair_in.at[p], chain_in.at[p])
        chain(p, 0, True).start()

    def relay_up(i):
        p = static_slot(i, 1)
        for own in (False, True):
            chain(p, 1, own).wait_recv()
            add(p, inner if own else other, chain_in.at[way(p, own)])

            @pl.when(jnp.logical_not(joins))
            def _():
                chain(p, 1, own).start()

            if not own:
                @pl.when(joins)
                def _():
                    pair(p).start()

    def join_up(i):
        @pl.when(joins)
        def _():
            p = static_slot(i, 1)
            pair(p).wait_recv()
            add(p, inner, pair_in.at[p])
            chain(p, 1, True).start()

    @pl.when(is_end)
    def _():
        gram = jnp.concatenate([whole[q] for q in range(n_row)], axis=0)

        strips = [2 + int(LEAD_PACE * i) for i in range(counts[0])]

        def between(strip):
            if strip in strips:
                @pl.when(final)
                def _():
                    lead(strips.index(strip))

        factor, inverse = factor_values(gram, top[...], between)
        factor_ref[...] = factor
        inverse_ref[:, :PANEL] = inverse
        inverse_ref[:, PANEL:] = dot_exact(inverse, factor, ((1,), (1,)))

        @pl.when(final)
        def _():
            for i in range(counts[0]):
                if strips[i] >= PANEL // STRIP:
                    lead(i)

        @pl.when(row == 0)
        def _():
            high, low = split(panel[:PANEL] + factor)
            shifted[:PANEL, :PANEL] = high
            shifted[:PANEL, PANEL:] = low

    def update(i):
        p = static_slot(i, 0)
        given(p).wait_recv()
        place = pl.ds(p * (2 * LANES), 2 * LANES)
        block[:, place] = block[:, place] - product(shifted, hold[:, place])

    def late(i, owner):
        p = static_slot(i, owner)

        @pl.when(row == 0)
        def _():
            place = unit(p, 1) if owner == 0 else lanes(p * (2 * LANES), 2 * LANES)
            extra = dot_exact(factor_ref[...], block[:PANEL, place], ((0,), (0,)))
            partial[:, place] = partial[:, place] + extra
            if owner == 0:
                pair(p).start()
            else:
                chain(p, 1, True).start()
                chain(p, 1, False).start()

    def solve(i, owner):
        p = static_slot(i, owner)
        pair(p).wait_recv()
        chain(p, owner, True).wait_recv()
        place = unit(p, inner)
        held = p >= prompt

        def at_row_zero():
            if held:
                top_in[i] = block[:PANEL, place]

        def elsewhere():
            if held:
                top_in[i] = jnp.zeros((PANEL, LANES), jnp.float32)
            else:
                send(top_in.at[i], top_in.at[i], scatter_send.at[0], scatter_recv.at[i], {"row": 0}).wait_recv()

        if owner == 0:
            pl.when(row == 0)(at_row_zero)
            pl.when(row != 0)(elsewhere)
        else:
            elsewhere()
        total = partial[:, place] + pair_in[p] + chain_in[p]
        hold[:, place] = dot_exact(inverse_ref[...], jnp.concatenate([total, top_in[i]], axis=0), ((1,), (0,)))
        onward(p, owner, True).start()
        give(p).start()

    def pass_other(i, owner):
        p = static_slot(i, owner)
        given(p).wait_recv()
        onward(p, owner, False).start()

    def accept(i, owner, own, stops):
        p = static_slot(i, owner)
        onward(p, owner, own).wait_recv()
        if not stops:
            onward(p, owner, own).start()
        if own and not is_direct(i, owner):
            give(p).start()

    turns = sorted((static_slot(i, owner), owner, i) for owner in range(2) for i in range(counts[owner]))

    def drain(sem, units):
        ref = partial.at[:, pl.ds(0, units * LANES)]
        send(ref, ref, sem.at[0], pair_recv.at[0], partner).wait_send()

    downs, ups = counts
    prompt_downs = sum(1 for p, owner, _ in turns if owner == 0 and p < prompt)
    prompt_ups = sum(1 for p, owner, _ in turns if owner == 1 and p < prompt)

    def settle(role):
        for p, owner, i in turns:
            if not is_direct(i, owner) and i >= UPDATES:
                given(p).wait_recv()
        drain(give_send, downs + (ups if role == 3 else 0))
        drain(pass_send, (downs, downs + 2 * ups, downs + 2 * ups, 2 * ups)[role])
        if role == 2:
            @pl.when(joins)
            def _():
                drain(pair_send, downs + ups)
                drain(chain_send, downs + ups)

            @pl.when(jnp.logical_not(joins))
            def _():
                drain(pair_send, downs)
                drain(chain_send, downs + 2 * ups)
        else:
            drain(pair_send, downs + (ups if role == 3 else 0))
            drain(chain_send, (2 * ups, downs + 2 * ups, 0, downs)[role])
        if role == 0:
            @pl.when(row == 0)
            def _():
                drain(scatter_send, prompt_downs + 2 * prompt_ups)

        @pl.when(col == 0)
        def _():
            for slot, c in enumerate(heads):
                panel_copy(c, slot).wait_send()
            send(arrived, arrived, part_send.at[0], part_recv.at[0], {"row": 0}).wait_send()
            sent = whole.at[pl.ds(0, 3 if role in (0, 3) else 4)]
            send(sent, sent, whole_send.at[0], whole_recv.at[0], {"row": 0}).wait_send()
            if role in (0, 3):
                drain(share_send, 2 * (n_col - 1))
            if role == 0:
                @pl.when(row == 0)
                def _():
                    drain(top_send, 3)

    def follow(role):
        if role == 0:
            @pl.when(row == 0)
            def _():
                kept = top_in.at[pl.ds(0, prompt_downs)]
                pltpu.make_async_copy(kept, kept, own_sem.at[0]).wait()

        for event in plan(role, counts, prompt):
            kind, owner, i = event
            if kind == "solve":
                solve(i, owner)
            elif kind == "late":
                late(i, owner)
            elif kind == "update":
                update(i)
            elif kind == "pass":
                pass_other(i, owner)
            elif kind == "down":
                relay_down(i)
            elif kind == "up":
                relay_up(i)
            elif kind == "join":
                join_up(i)
            else:
                accept(i, owner, kind == "own", role == (3, 0)[owner])
        settle(role)

    pl.when(first)(lambda: follow(0))
    pl.when(jnp.logical_not(is_end) & (near == 0))(lambda: follow(1))
    pl.when(jnp.logical_not(is_end) & (near == 1))(lambda: follow(2))
    pl.when(final)(lambda: follow(3))


def flush_kernel(n_up, block, hold, shifted, out, ring, sem, done_sem):
    slots = ring.shape[0]
    rest = out.shape[1] // (2 * LANES) - UPDATES

    def lanes(p):
        return pl.ds(p * (2 * LANES) if isinstance(p, int) else pl.multiple_of(p * (2 * LANES), LANES), 2 * LANES)

    def place(r):
        return lanes(jnp.where(r < n_up, 2 * r + 1, r + UPDATES))

    def store(r):
        slot = lax.rem(r, slots)
        return pltpu.make_async_copy(ring.at[slot], out.at[:, place(r)], sem.at[slot])

    def done(i):
        where = lanes(slot_of(i, 0, n_up))
        return pltpu.make_async_copy(block.at[:, where], out.at[:, where], done_sem.at[i])

    for i in range(UPDATES):
        done(i).start()

    @pl.loop(0, rest)
    def _(r):
        @pl.when(r >= slots)
        def _():
            store(r - slots).wait()

        ring[lax.rem(r, slots)] = block[:, place(r)] - product(shifted, hold[:, place(r)])
        store(r).start()

    for i in range(UPDATES):
        done(i).wait()

    @pl.loop(rest - slots, rest)
    def _(r):
        store(r).wait()


def flush(block, hold, shifted, n_up):
    height, width = block.shape
    vmem = pl.BlockSpec(memory_space=pltpu.VMEM)
    return pl.pallas_call(
        functools.partial(flush_kernel, n_up),
        out_shape=jax.ShapeDtypeStruct(block.shape, block.dtype),
        in_specs=[vmem] * 3,
        out_specs=pl.BlockSpec(memory_space=pl.ANY),
        scratch_shapes=[
            pltpu.VMEM((4, height, 2 * LANES), jnp.float32),
            pltpu.SemaphoreType.DMA((4,)),
            pltpu.SemaphoreType.DMA((UPDATES,)),
        ],
        compiler_params=pltpu.CompilerParams(vmem_limit_bytes=16 * 1024 * 1024),
        name="flush",
    )(block, hold, shifted)


def on_device(n_row, n_col, matrix):
    height, width = matrix.shape
    piece = PANEL // n_row
    blocks = width // (4 * LANES)
    pairs = 2 * blocks
    most, ups = owned_counts(pairs)
    dma = pltpu.SemaphoreType.DMA
    f32, bf16 = jnp.float32, jnp.bfloat16
    block, hold, shifted = pl.pallas_call(
        functools.partial(step_kernel, n_row, n_col),
        out_shape=(
            jax.ShapeDtypeStruct((height, width), f32),
            jax.ShapeDtypeStruct((PANEL, width), f32),
            jax.ShapeDtypeStruct((height, 2 * PANEL), bf16),
        ),
        in_specs=[pl.BlockSpec(memory_space=pltpu.HBM)],
        out_specs=(pl.BlockSpec(memory_space=pltpu.VMEM),) * 3,
        scratch_shapes=[
            pltpu.VMEM((PANEL, width), f32),
            pltpu.VMEM((pairs, PANEL, LANES), f32),
            pltpu.VMEM((pairs + ups, PANEL, LANES), f32),
            pltpu.VMEM((most, PANEL, LANES), f32),
            pltpu.VMEM((2 * PANEL, height), bf16),
            pltpu.VMEM((height, PANEL), f32),
            pltpu.VMEM((PANEL, PANEL), f32),
            pltpu.VMEM((PANEL, PANEL), f32),
            pltpu.VMEM((PANEL, 2 * PANEL), f32),
            pltpu.VMEM((n_row, piece, PANEL), f32),
            pltpu.VMEM((n_row - 1, piece, PANEL), f32),
            pltpu.VMEM((n_row, piece, PANEL), f32),
            dma((1,)),
            dma((blocks,)),
            dma((1,)),
            dma((n_col,)),
            dma((1,)),
            dma((1,)),
            dma((1,)),
            dma((1,)),
            dma((1,)),
            dma((1,)),
            dma((1,)),
            dma((1,)),
            dma((2,)),
            dma((1,)),
            dma((most,)),
            dma((1,)),
            dma((pairs,)),
            dma((1,)),
            dma((pairs + ups,)),
            dma((1,)),
            dma((pairs,)),
            dma((1,)),
            dma((pairs + ups,)),
        ],
        compiler_params=pltpu.CompilerParams(
            collective_id=0, has_side_effects=True, vmem_limit_bytes=36 * 1024 * 1024
        ),
        name="whole_step",
    )(matrix)
    return flush(block, hold, shifted, owned_counts(pairs)[1])


def solution(mesh):
    body = functools.partial(on_device, mesh.shape["row"], mesh.shape["col"])
    return jax.shard_map(body, mesh=mesh, in_specs=(P("row", "col"),), out_specs=P("row", "col"), check_vma=False)
```

```python
import functools

import jax
import jax.numpy as jnp
from jax import lax
from jax.experimental import pallas as pl
from jax.experimental.pallas import tpu as pltpu
from jax.sharding import PartitionSpec as P

PANEL = 128
STRIP = 8
LANES = 128
MESH = pl.DeviceIdType.MESH
EARLY = 8
LATE = 7
UP_SHARE = 5
UPDATES = 6
LEAD_PACE = 1.6
HOP = 4.1
UPDATE_LAG = 8.5


def dot_exact(a, b, contract):
    return lax.dot_general(
        a, b, (contract, ((), ())), precision=lax.Precision.HIGHEST, preferred_element_type=jnp.float32
    )


def factor_values(gram, top, between=lambda strip: None):
    strips = PANEL // STRIP
    shape = (STRIP, LANES)
    rows = lax.broadcasted_iota(jnp.int32, shape, 0)
    lanes = lax.broadcasted_iota(jnp.int32, shape, 1)
    eye = (
        lax.broadcasted_iota(jnp.int32, (PANEL, PANEL), 0) == lax.broadcasted_iota(jnp.int32, (PANEL, PANEL), 1)
    ).astype(jnp.float32)
    chol = jnp.concatenate([gram, eye], axis=1)
    work = jnp.concatenate([top, jnp.zeros_like(top)], axis=1)
    factor_rows = []
    previous = None

    def spread(x, start):
        return [jnp.broadcast_to(x[:, start + c : start + c + 1], shape) for c in range(STRIP)]

    for strip in range(strips + 1):
        at, back = strip * STRIP, (strip - 1) * STRIP
        if strip < strips:
            between(strip)
            panel = chol[:STRIP]
            columns = spread(panel, at)
            halves = [panel[:, :LANES], panel[:, LANES:]]
            scale = jnp.ones(shape, jnp.float32)
        if strip > 0:
            inner = work[back : back + STRIP] + previous
            aside = work[:, back : back + STRIP]
            inner_columns = spread(inner, back)
            inner_halves = [inner[:, :LANES], inner[:, LANES:]]
        for j in range(STRIP):
            if strip < strips:
                pivot = columns[j][j : j + 1]
                multiplier = jnp.where(rows > j, columns[j] * (1.0 / pivot), 0.0)
                scale = jnp.where(rows == j, lax.rsqrt(pivot), scale)
                columns = [x if c <= j else x - multiplier * x[j : j + 1] for c, x in enumerate(columns)]
                halves = [x - multiplier * x[j : j + 1] for x in halves]
            if strip > 0:
                column = inner_columns[j]
                inverse = 1.0 / column[j : j + 1]

                def eliminate(x):
                    pivot_row = x[j : j + 1] * inverse
                    return jnp.where(rows == j, pivot_row, x - column * pivot_row)

                inner_columns = [x if c <= j else eliminate(x) for c, x in enumerate(inner_columns)]
                inner_halves = [eliminate(x) for x in inner_halves]
        if strip < strips:
            halves = [halves[0] * scale, halves[1] * scale]
            halves[0] = jnp.where(lanes >= at + rows, halves[0], 0.0)
            panel = jnp.concatenate(halves, axis=1)
            factor_rows.append(halves[0])
            if strip < strips - 1:
                chol = chol[STRIP:] - dot_exact(panel[:, at + STRIP : PANEL], panel, ((0,), (0,)))
        if strip > 0:
            inner = jnp.concatenate(inner_halves, axis=1)
            update = dot_exact(aside, inner, ((1,), (0,)))
            pieces = []
            if back > 0:
                pieces.append(work[:back] - update[:back])
            pieces.append(inner)
            if strip < strips:
                pieces.append(work[at:] - update[at:])
            work = jnp.concatenate(pieces, axis=0)
        previous = panel
    return jnp.concatenate(factor_rows, axis=0), work[:, PANEL:]


def send(src, dst, send_sem, recv_sem, target):
    return pltpu.make_async_remote_copy(
        src_ref=src, dst_ref=dst, send_sem=send_sem, recv_sem=recv_sem, device_id=target, device_id_type=MESH
    )


def split(x):
    high = x.astype(jnp.bfloat16)
    return high, (x - high.astype(jnp.float32)).astype(jnp.bfloat16)


def product(shifted, values):
    high, low = split(values)
    both = jnp.dot(shifted[...], jnp.concatenate([high, high], axis=0), preferred_element_type=jnp.float32)
    return both + jnp.dot(shifted[:, :PANEL], low, preferred_element_type=jnp.float32)


def owned_counts(pairs):
    return pairs - pairs // UP_SHARE, pairs // UP_SHARE


def slot_of(i, owner, n_up):
    if owner == 1:
        return 2 * i + 1
    return 2 * i if i < n_up else i + n_up


def is_direct(i, owner):
    return owner == 1


def plan(role, counts, prompt):
    events = []

    def put(time, kind, owner, i):
        events.append((time, len(events), (kind, owner, i)))

    held = [0, 0]
    turns = sorted((slot_of(i, owner, counts[1]), owner, i) for owner in range(2) for i in range(counts[owner]))
    for p, owner, i in turns:
        after = held[owner]
        if p >= prompt:
            held[owner] += 1
            if role == 0:
                put(26.0 + 0.1 * i if owner == 1 else 27.0 + 0.7 * after, "late", owner, i)
        if owner == 0:
            sent = 31.4 + 1.5 * i
            if i < UPDATES:
                put(47.0 + i if role == 0 else sent + HOP * role + UPDATE_LAG, "update", 0, i)
            if role == 0:
                put(27.3 + 0.7 * i, "solve", 0, i)
            else:
                put(sent + HOP * role, "own", 0, i)
            if role in (1, 2):
                put(21.2 + 1.4 * i + 3.2 * (2 - role), "down", 0, i)
            continue
        near, away, join, solved = 25.0 + 2.8 * i, 29.0 + 2.8 * i, 33.0 + 2.8 * i, 37.0 + 2.4 * i
        if p >= prompt:
            near, away, join, solved = 34.0 + 3.5 * after, 37.5 + 3.5 * after, 41.0 + 3.5 * after, 46.0 + 3.0 * after
        if role == 3:
            put(solved, "solve", 1, i)
            put(solved + 8.0, "pass", 1, i)
        else:
            put(solved + 1.5 + HOP * (3 - role), "own", 1, i)
            put(solved + 5.0 + HOP * (4 - role), "other", 1, i)
        if role == 1:
            put(near, "up", 1, i)
        if role == 2:
            put(away, "up", 1, i)
            put(join, "join", 1, i)
    return [event for _, _, event in sorted(events)]


def step_kernel(
    n_row, n_col, matrix_ref, block, hold, shifted,
    partial, pair_in, chain_in, top_in, stacked, panel, top, factor_ref, inverse_ref,
    parts, arrived, whole,
    go_sem, fetch_sem, block_sem, own_sem,
    panel_send, panel_recv, part_send, part_recv, whole_send, whole_recv, top_send, top_recv, share_send, share_recv,
    scatter_send, scatter_recv, pair_send, pair_recv, chain_send, chain_recv,
    give_send, give_recv, pass_send, pass_recv,
):
    row, col = lax.axis_index("row"), lax.axis_index("col")
    width = block.shape[1]
    blocks = width // (4 * LANES)
    pairs = 2 * blocks
    counts = owned_counts(pairs)
    prompt = pairs - LATE
    piece = PANEL // n_row
    outer_n = n_row // 2
    last = outer_n - 1
    outer, inner = row // 2, lax.rem(row, 2)
    other = 1 - inner
    partner = {"row": outer * 2 + other}
    first, final = outer == 0, outer == last
    is_end = first | final
    mine = jnp.where(first, 0, 1)
    near = jnp.where(2 * outer < outer_n, 0, 1)
    end_rows = [0, 1, n_row - 2, n_row - 1]

    barrier = pltpu.get_barrier_semaphore()
    for d in range(1, n_row):
        pl.semaphore_signal(barrier, inc=1, device_id={"row": lax.rem(row + d, n_row)}, device_id_type=MESH)
    for d in range(1, n_col):
        pl.semaphore_signal(barrier, inc=1, device_id={"col": lax.rem(col + d, n_col)}, device_id_type=MESH)

    def lanes(start, size):
        return pl.ds(pl.multiple_of(start, LANES), size)

    def unit(p, side):
        return lanes(p * (2 * LANES) + side * LANES, LANES)

    def load(j):
        place = lanes(j * (4 * LANES), 4 * LANES)
        return pltpu.make_async_copy(matrix_ref.at[:, place], block.at[:, place], block_sem.at[j])

    def static_slot(i, owner):
        return slot_of(i, owner, counts[1])

    def owner_of(p):
        return jnp.where((p < 2 * counts[1]) & (lax.rem(p, 2) == 1), 1, 0)

    def turn_of(p):
        if isinstance(p, int):
            return p // 2 if p < 2 * counts[1] else p - counts[1]
        return jnp.where(p < 2 * counts[1], lax.div(p, 2), p - counts[1])

    def scatter(p, side, up):
        return send(
            matrix_ref.at[pl.ds(0, PANEL), unit(p, side)], top_in.at[turn_of(p)],
            scatter_send.at[0], scatter_recv.at[turn_of(p)], {"row": end_rows[2 * up + side]},
        )

    def keep(i):
        place = unit(static_slot(i, 0), 0)
        return pltpu.make_async_copy(matrix_ref.at[pl.ds(0, PANEL), place], top_in.at[i], own_sem.at[0])

    def start_scatter(p):
        @pl.when((row == 0) & (owner_of(p) == 0) & (p < prompt))
        def _():
            scatter(p, 1, 0).start()

    def start_up(i):
        @pl.when((row == 0) & (static_slot(i, 1) < prompt))
        def _():
            for side in range(2):
                scatter(static_slot(i, 1), side, 1).start()

    def pair(p):
        return send(partial.at[:, unit(p, other)], pair_in.at[p], pair_send.at[0], pair_recv.at[p], partner)

    def chain(p, towards, own):
        slot = way(p, own)
        return send(
            partial.at[:, unit(p, inner if own else other)], chain_in.at[slot],
            chain_send.at[0], chain_recv.at[slot], {"row": row + 2 * (2 * towards - 1)},
        )

    def way(p, own):
        return p if own else pairs + turn_of(p)

    joins = outer == last - 1

    def give(p):
        place = unit(p, inner)
        return send(hold.at[:, place], hold.at[:, place], give_send.at[0], give_recv.at[p], partner)

    def given(p):
        place = unit(p, other)
        return send(hold.at[:, place], hold.at[:, place], give_send.at[0], give_recv.at[p], partner)

    def onward(p, owner, own):
        place = unit(p, inner if own else other)
        slot = way(p, own)
        return send(
            hold.at[:, place], hold.at[:, place], pass_send.at[0], pass_recv.at[slot],
            {"row": row + 2 * (1 - 2 * owner)},
        )

    def multiply(j):
        place = lanes(j * (4 * LANES), 4 * LANES)
        high, low = split(block[:, place])
        both = jnp.dot(stacked[...], high, preferred_element_type=jnp.float32)
        rest = jnp.dot(stacked[:PANEL], low, preferred_element_type=jnp.float32)
        partial[:, place] = both[:PANEL] + both[PANEL:] + rest

    def exchange(p):
        owner = owner_of(p)

        prompt_here = jnp.logical_not((row == 0) & (p >= prompt))

        @pl.when((owner == 0) & prompt_here)
        def _():
            pair(p).start()

        @pl.when((owner == 1) & first & prompt_here)
        def _():
            chain(p, owner, True).start()
            chain(p, owner, False).start()

    def exchange_last():
        @pl.when(final)
        def _():
            for i in range(counts[1]):
                pair(static_slot(i, 1)).start()

    def prepare():
        high, low = split(panel[...])
        shifted[:, :PANEL] = high
        shifted[:, PANEL:] = low
        high, low = split(jnp.transpose(panel[...]))
        stacked[:PANEL] = high
        stacked[PANEL:] = low

    def multiply_range(start, stop, ahead):
        @pl.loop(start, stop)
        def _(j):
            load(j).wait()
            multiply(j)
            for p in (2 * j, 2 * j + 1):
                exchange(p)

                @pl.when(p + ahead < pairs)
                def _():
                    start_scatter(p + ahead)

    @pl.when(col == 0)
    def _():
        fetch = pltpu.make_async_copy(matrix_ref.at[:, pl.ds(0, PANEL)], panel, fetch_sem.at[0])
        fetch.start()
        fetch.wait()
        for j in range(blocks):
            load(j).start()
        local = dot_exact(panel[...], panel[...], ((0,), (0,)))
        for q in range(n_row):
            parts[q] = local[q * piece : (q + 1) * piece]

    @pl.when(col != 0)
    def _():
        for j in range(blocks):
            load(j).start()

    @pl.when(row == 0)
    def _():
        for i in range(counts[0]):
            if static_slot(i, 0) < prompt:
                keep(i).start()

    pl.semaphore_wait(barrier, n_row - 1 + n_col - 1)

    def panel_copy(to, slot):
        return send(panel, panel, panel_send.at[slot], panel_recv.at[0], {"col": to})

    heads = [1] + [c for c in range(2, n_col, 2)]

    @pl.when(col == 0)
    def _():
        def part(d):
            q = lax.rem(row + d, n_row)
            return send(parts.at[q], arrived.at[d - 1], part_send.at[0], part_recv.at[0], {"row": q})

        def whole_copy(e):
            return send(whole.at[row], whole.at[row], whole_send.at[0], whole_recv.at[0], {"row": end_rows[e]})

        def top_copy(e):
            return send(panel.at[pl.ds(0, PANEL)], top, top_send.at[0], top_recv.at[0], {"row": end_rows[e]})

        def share(c, slot):
            ref = (top, whole)[slot]
            return send(ref, ref, share_send.at[0], share_recv.at[slot], {"col": c})

        for d in range(1, n_row):
            part(d).start()
        for slot, c in enumerate(heads):
            panel_copy(c, slot).start()

        @pl.when(row == 0)
        def _():
            for e in range(1, 4):
                top_copy(e).start()
            top[...] = panel[:PANEL]

        prepare()

        @pl.loop(0, blocks // 2)
        def _(j):
            load(j).wait()
            multiply(j)

        send(arrived, arrived, part_send.at[0], part_recv.at[0], {"row": 0}).wait_recv()
        total = parts[row]
        for d in range(1, n_row):
            total = total + arrived[d - 1]
        whole[row] = total
        for e in range(4):
            @pl.when(row != end_rows[e])
            def _():
                whole_copy(e).start()

        pl.semaphore_signal(go_sem, inc=1, device_id={"col": 1}, device_id_type=MESH)
        for i in range(counts[1]):
            start_up(i)

        @pl.loop(0, 2 * (blocks // 2))
        def _(p):
            exchange(p)

            start_scatter(p)

        @pl.when(is_end)
        def _():
            @pl.when(row != 0)
            def _():
                send(top, top, top_send.at[0], top_recv.at[0], {"row": 0}).wait_recv()

            for c in range(1, n_col):
                share(c, 0).start()

        multiply_range(blocks // 2, blocks, 0)
        exchange_last()

        @pl.when(is_end)
        def _():
            most = whole.at[pl.ds(0, n_row - 1)]
            send(most, most, whole_send.at[0], whole_recv.at[0], {"row": 0}).wait_recv()
            for c in range(1, n_col):
                share(c, 1).start()

    @pl.when(col != 0)
    def _():
        @pl.when(col != 1)
        def _():
            for p in range(EARLY):
                start_scatter(p)
            for i in range(counts[1]):
                start_up(i)

        root = {"col": 0}
        send(panel, panel, panel_send.at[0], panel_recv.at[0], root).wait_recv()
        relay = (lax.rem(col, 2) == 0) & (col + 1 < n_col)

        @pl.when(relay)
        def _():
            panel_copy(col + 1, 0).start()

        prepare()

        @pl.when(col == 1)
        def _():
            @pl.loop(0, blocks)
            def _(j):
                load(j).wait()
                multiply(j)

            pl.semaphore_wait(go_sem, 1)
            for i in range(counts[1]):
                start_up(i)

            @pl.loop(0, pairs)
            def _(p):
                exchange(p)
                start_scatter(p)

        @pl.when(col != 1)
        def _():
            multiply_range(0, blocks, EARLY)

        exchange_last()

        @pl.when(is_end)
        def _():
            send(top, top, share_send.at[0], share_recv.at[0], root).wait_recv()
            send(whole, whole, share_send.at[0], share_recv.at[1], root).wait_recv()

        @pl.when(relay)
        def _():
            panel_copy(col + 1, 0).wait_send()

    def add(p, side, *terms):
        place = unit(p, side)
        total = partial[:, place]
        for term in terms:
            total = total + term[...]
        partial[:, place] = total

    def lead(i):
        p = static_slot(i, 0)
        pair(p).wait_recv()
        add(p, inner, pair_in.at[p])
        chain(p, 0, True).start()

    def relay_down(i):
        p = static_slot(i, 0)
        pair(p).wait_recv()
        chain(p, 0, True).wait_recv()
        add(p, inner, pair_in.at[p], chain_in.at[p])
        chain(p, 0, True).start()

    def relay_up(i):
        p = static_slot(i, 1)
        for own in (False, True):
            chain(p, 1, own).wait_recv()
            add(p, inner if own else other, chain_in.at[way(p, own)])

            @pl.when(jnp.logical_not(joins))
            def _():
                chain(p, 1, own).start()

            if not own:
                @pl.when(joins)
                def _():
                    pair(p).start()

    def join_up(i):
        @pl.when(joins)
        def _():
            p = static_slot(i, 1)
            pair(p).wait_recv()
            add(p, inner, pair_in.at[p])
            chain(p, 1, True).start()

    @pl.when(is_end)
    def _():
        gram = jnp.concatenate([whole[q] for q in range(n_row)], axis=0)

        strips = [2 + int(LEAD_PACE * i) for i in range(counts[0])]

        def between(strip):
            if strip in strips:
                @pl.when(final)
                def _():
                    lead(strips.index(strip))

        factor, inverse = factor_values(gram, top[...], between)
        factor_ref[...] = factor
        inverse_ref[:, :PANEL] = inverse
        inverse_ref[:, PANEL:] = dot_exact(inverse, factor, ((1,), (1,)))

        @pl.when(final)
        def _():
            for i in range(counts[0]):
                if strips[i] >= PANEL // STRIP:
                    lead(i)

        @pl.when(row == 0)
        def _():
            high, low = split(panel[:PANEL] + factor)
            shifted[:PANEL, :PANEL] = high
            shifted[:PANEL, PANEL:] = low

    def update(i):
        p = static_slot(i, 0)
        given(p).wait_recv()
        place = pl.ds(p * (2 * LANES), 2 * LANES)
        block[:, place] = block[:, place] - product(shifted, hold[:, place])

    def late(i, owner):
        p = static_slot(i, owner)

        @pl.when(row == 0)
        def _():
            place = unit(p, 1) if owner == 0 else lanes(p * (2 * LANES), 2 * LANES)
            extra = dot_exact(factor_ref[...], block[:PANEL, place], ((0,), (0,)))
            partial[:, place] = partial[:, place] + extra
            if owner == 0:
                pair(p).start()
            else:
                chain(p, 1, True).start()
                chain(p, 1, False).start()

    def solve(i, owner):
        p = static_slot(i, owner)
        pair(p).wait_recv()
        chain(p, owner, True).wait_recv()
        place = unit(p, inner)
        held = p >= prompt

        def at_row_zero():
            if held:
                top_in[i] = block[:PANEL, place]

        def elsewhere():
            if held:
                top_in[i] = jnp.zeros((PANEL, LANES), jnp.float32)
            else:
                send(top_in.at[i], top_in.at[i], scatter_send.at[0], scatter_recv.at[i], {"row": 0}).wait_recv()

        if owner == 0:
            pl.when(row == 0)(at_row_zero)
            pl.when(row != 0)(elsewhere)
        else:
            elsewhere()
        total = partial[:, place] + pair_in[p] + chain_in[p]
        hold[:, place] = dot_exact(inverse_ref[...], jnp.concatenate([total, top_in[i]], axis=0), ((1,), (0,)))
        onward(p, owner, True).start()
        give(p).start()

    def pass_other(i, owner):
        p = static_slot(i, owner)
        given(p).wait_recv()
        onward(p, owner, False).start()

    def accept(i, owner, own, stops):
        p = static_slot(i, owner)
        onward(p, owner, own).wait_recv()
        if not stops:
            onward(p, owner, own).start()
        if own and not is_direct(i, owner):
            give(p).start()

    turns = sorted((static_slot(i, owner), owner, i) for owner in range(2) for i in range(counts[owner]))

    def drain(sem, units):
        ref = partial.at[:, pl.ds(0, units * LANES)]
        send(ref, ref, sem.at[0], pair_recv.at[0], partner).wait_send()

    downs, ups = counts
    prompt_downs = sum(1 for p, owner, _ in turns if owner == 0 and p < prompt)
    prompt_ups = sum(1 for p, owner, _ in turns if owner == 1 and p < prompt)

    def settle(role):
        for p, owner, i in turns:
            if not is_direct(i, owner) and i >= UPDATES:
                given(p).wait_recv()
        drain(give_send, downs + (ups if role == 3 else 0))
        drain(pass_send, (downs, downs + 2 * ups, downs + 2 * ups, 2 * ups)[role])
        if role == 2:
            @pl.when(joins)
            def _():
                drain(pair_send, downs + ups)
                drain(chain_send, downs + ups)

            @pl.when(jnp.logical_not(joins))
            def _():
                drain(pair_send, downs)
                drain(chain_send, downs + 2 * ups)
        else:
            drain(pair_send, downs + (ups if role == 3 else 0))
            drain(chain_send, (2 * ups, downs + 2 * ups, 0, downs)[role])
        if role == 0:
            @pl.when(row == 0)
            def _():
                drain(scatter_send, prompt_downs + 2 * prompt_ups)

        @pl.when(col == 0)
        def _():
            for slot, c in enumerate(heads):
                panel_copy(c, slot).wait_send()
            send(arrived, arrived, part_send.at[0], part_recv.at[0], {"row": 0}).wait_send()
            sent = whole.at[pl.ds(0, 3 if role in (0, 3) else 4)]
            send(sent, sent, whole_send.at[0], whole_recv.at[0], {"row": 0}).wait_send()
            if role in (0, 3):
                drain(share_send, 2 * (n_col - 1))
            if role == 0:
                @pl.when(row == 0)
                def _():
                    drain(top_send, 3)

    def follow(role):
        if role == 0:
            @pl.when(row == 0)
            def _():
                kept = top_in.at[pl.ds(0, prompt_downs)]
                pltpu.make_async_copy(kept, kept, own_sem.at[0]).wait()

        for event in plan(role, counts, prompt):
            kind, owner, i = event
            if kind == "solve":
                solve(i, owner)
            elif kind == "late":
                late(i, owner)
            elif kind == "update":
                update(i)
            elif kind == "pass":
                pass_other(i, owner)
            elif kind == "down":
                relay_down(i)
            elif kind == "up":
                relay_up(i)
            elif kind == "join":
                join_up(i)
            else:
                accept(i, owner, kind == "own", role == (3, 0)[owner])
        settle(role)

    pl.when(first)(lambda: follow(0))
    pl.when(jnp.logical_not(is_end) & (near == 0))(lambda: follow(1))
    pl.when(jnp.logical_not(is_end) & (near == 1))(lambda: follow(2))
    pl.when(final)(lambda: follow(3))


def flush_kernel(n_up, block, hold, shifted, out, ring, sem, done_sem):
    slots = ring.shape[0]
    rest = out.shape[1] // (2 * LANES) - UPDATES

    def lanes(p):
        return pl.ds(p * (2 * LANES) if isinstance(p, int) else pl.multiple_of(p * (2 * LANES), LANES), 2 * LANES)

    def place(r):
        return lanes(jnp.where(r < n_up, 2 * r + 1, r + UPDATES))

    def store(r):
        slot = lax.rem(r, slots)
        return pltpu.make_async_copy(ring.at[slot], out.at[:, place(r)], sem.at[slot])

    def done(i):
        where = lanes(slot_of(i, 0, n_up))
        return pltpu.make_async_copy(block.at[:, where], out.at[:, where], done_sem.at[i])

    for i in range(UPDATES):
        done(i).start()

    @pl.loop(0, rest)
    def _(r):
        @pl.when(r >= slots)
        def _():
            store(r - slots).wait()

        ring[lax.rem(r, slots)] = block[:, place(r)] - product(shifted, hold[:, place(r)])
        store(r).start()

    for i in range(UPDATES):
        done(i).wait()

    @pl.loop(rest - slots, rest)
    def _(r):
        store(r).wait()


def flush(block, hold, shifted, n_up):
    height, width = block.shape
    vmem = pl.BlockSpec(memory_space=pltpu.VMEM)
    return pl.pallas_call(
        functools.partial(flush_kernel, n_up),
        out_shape=jax.ShapeDtypeStruct(block.shape, block.dtype),
        in_specs=[vmem] * 3,
        out_specs=pl.BlockSpec(memory_space=pl.ANY),
        scratch_shapes=[
            pltpu.VMEM((4, height, 2 * LANES), jnp.float32),
            pltpu.SemaphoreType.DMA((4,)),
            pltpu.SemaphoreType.DMA((UPDATES,)),
        ],
        compiler_params=pltpu.CompilerParams(vmem_limit_bytes=16 * 1024 * 1024),
        name="flush",
    )(block, hold, shifted)


def on_device(n_row, n_col, matrix):
    height, width = matrix.shape
    piece = PANEL // n_row
    blocks = width // (4 * LANES)
    pairs = 2 * blocks
    most, ups = owned_counts(pairs)
    dma = pltpu.SemaphoreType.DMA
    f32, bf16 = jnp.float32, jnp.bfloat16
    block, hold, shifted = pl.pallas_call(
        functools.partial(step_kernel, n_row, n_col),
        out_shape=(
            jax.ShapeDtypeStruct((height, width), f32),
            jax.ShapeDtypeStruct((PANEL, width), f32),
            jax.ShapeDtypeStruct((height, 2 * PANEL), bf16),
        ),
        in_specs=[pl.BlockSpec(memory_space=pltpu.HBM)],
        out_specs=(pl.BlockSpec(memory_space=pltpu.VMEM),) * 3,
        scratch_shapes=[
            pltpu.VMEM((PANEL, width), f32),
            pltpu.VMEM((pairs, PANEL, LANES), f32),
            pltpu.VMEM((pairs + ups, PANEL, LANES), f32),
            pltpu.VMEM((most, PANEL, LANES), f32),
            pltpu.VMEM((2 * PANEL, height), bf16),
            pltpu.VMEM((height, PANEL), f32),
            pltpu.VMEM((PANEL, PANEL), f32),
            pltpu.VMEM((PANEL, PANEL), f32),
            pltpu.VMEM((PANEL, 2 * PANEL), f32),
            pltpu.VMEM((n_row, piece, PANEL), f32),
            pltpu.VMEM((n_row - 1, piece, PANEL), f32),
            pltpu.VMEM((n_row, piece, PANEL), f32),
            pltpu.SemaphoreType.REGULAR,
            dma((1,)),
            dma((blocks,)),
            dma((1,)),
            dma((n_col,)),
            dma((1,)),
            dma((1,)),
            dma((1,)),
            dma((1,)),
            dma((1,)),
            dma((1,)),
            dma((1,)),
            dma((1,)),
            dma((2,)),
            dma((1,)),
            dma((most,)),
            dma((1,)),
            dma((pairs,)),
            dma((1,)),
            dma((pairs + ups,)),
            dma((1,)),
            dma((pairs,)),
            dma((1,)),
            dma((pairs + ups,)),
        ],
        compiler_params=pltpu.CompilerParams(
            collective_id=0, has_side_effects=True, vmem_limit_bytes=36 * 1024 * 1024
        ),
        name="whole_step",
    )(matrix)
    return flush(block, hold, shifted, owned_counts(pairs)[1])


def solution(mesh):
    body = functools.partial(on_device, mesh.shape["row"], mesh.shape["col"])
    return jax.shard_map(body, mesh=mesh, in_specs=(P("row", "col"),), out_specs=P("row", "col"), check_vma=False)
```
